512 devices in a mesh: gx: 32 (over y, x_lo, core), gy: 16 (over z, x_hi).
Axes of the slice: x: 4 (x_hi: 2, x_lo: 2; x = x_hi * 2 + x_lo), y: 8, z: 8, core: 2. Of those that a mesh axis runs over, the one named last changes fastest.
Arguments:
- electric: float32 [3, 16, 256, 2048], P(None, None, 'gx', 'gy'), may hold values from -6 to 6
- magnetic: float32 [3, 16, 256, 2048], P(None, None, 'gx', 'gy'), may hold values from -6 to 6
- material: int32 [16, 256, 2048], P(None, 'gx', 'gy'), may hold values from 0 to 3
- permittivity: float32 [4], replicated, may hold values from 1 to 12
- slab_spectra: float32 [2, 128, 256, 2048], P(None, None, 'gx', 'gy'), may hold values from -6 to 6
- monitor_spectra: float32 [16, 2, 4, 256, 2048], P(None, None, None, 'gx', 'gy'), may hold values from -6 to 6
- wave_index: int32 [16], replicated, may hold values from 0 to 63
Outputs:
- electric_next: float32 [3, 16, 256, 2048], P(None, None, 'gx', 'gy')
- magnetic_next: float32 [3, 16, 256, 2048], P(None, None, 'gx', 'gy')
- slab_next: float32 [2, 128, 256, 2048], P(None, None, 'gx', 'gy')
- monitor_next: float32 [16, 2, 4, 256, 2048], P(None, None, None, 'gx', 'gy')
- orders: float32 [16, 2, 4, 128, 64], P('gy', None, None, 'gx')
The draws below stay inside these ranges and needn't reach their ends.
All inputs are finite; a program needn't handle non-finite values.
Results may differ from the reference program's by a relative error of at most 0.00007.
Values sent between devices are 32-bit elements; how exact they have to be, the bound alone decides.
A program may use at most 64 MiB of HBM per device.

```python
import math
import jax
import jax.numpy as jnp
from jax import lax

NF = 64
NW = 16
OY = 128
OX = 64
CLASSES = 4
NX = 256
NY = 2048
NZ = 16


def with_ends(entries, rng, smallest, top_value):
    longest = entries.shape.index(max(entries.shape))
    spots = []
    for shift in (0, 1):
        where = [jax.random.randint(jax.random.fold_in(rng, axis), (), 0, length) for axis, length in enumerate(entries.shape)]
        where[longest] = (where[longest] + shift) % entries.shape[longest]
        spots.append(tuple(where))
    return entries.at[spots[0]].set(smallest).at[spots[1]].set(top_value)


def raised(result, stream_key, source, target, parts, factor):
    owner, partner = [(jnp.arange(result.shape[axis_at]) // (result.shape[axis_at] // parts)).reshape([-1 if axis == axis_at else 1 for axis in range(result.ndim)]) for axis_at in (source, target)]
    chosen = jax.random.permutation(stream_key, parts)[partner]
    strong = (owner == chosen) | (owner == (partner + parts // 2) % parts)
    return jnp.where(strong, factor * result, result)


def level_of(own_key, extent, shards, least, largest):
    def one(axis_at, parts):
        steps = jax.random.uniform(jax.random.fold_in(jax.random.fold_in(own_key, 6), axis_at), (parts,), jnp.float32, least / len(shards), largest / len(shards))
        return jnp.repeat(jnp.exp(steps), extent[axis_at] // parts).reshape((-1,) + (1,) * (len(extent) - axis_at - 1))

    factor_of = one(*shards[0])
    for cut in shards[1:]:
        factor_of = factor_of * one(*cut)
    return factor_of


def scatter_about(stream_key, extent, width, most, pieces=(), held_as=jnp.bfloat16):
    values = width * jax.random.normal(stream_key, extent, jnp.float32)
    if pieces:
        values = values * level_of(stream_key, extent, pieces, -0.22, 0.18)
    return jnp.clip(values, -most, most).astype(held_as)


def heavy_noise(key, dims, spread, most, shards, heavy, kind=jnp.bfloat16):
    result = spread * jax.random.normal(key, dims, jnp.float32)
    if shards:
        result = result * level_of(key, dims, shards, -0.22, 0.18)
    return jnp.clip(raised(result, jax.random.fold_in(key, 3), *heavy), -most, most).astype(kind)


def setup_inputs(seed: int = 0) -> dict:
    seeds = jax.random.split(jax.random.key(seed), 8)
    electric = scatter_about(seeds[0], (3, NZ, NX, NY), 1.0, 6.0, ((2, 32), (3, 16)), jnp.float32)
    magnetic = scatter_about(seeds[1], (3, NZ, NX, NY), 1.0, 6.0, ((2, 32), (3, 16)), jnp.float32)
    material = with_ends(jax.random.randint(seeds[2], (NZ, NX, NY), 0, CLASSES), jax.random.fold_in(seeds[2], 1), 0, CLASSES - 1).astype(jnp.int32)
    permittivity = jnp.clip(jnp.exp(jax.random.uniform(seeds[3], (CLASSES,), jnp.float32, math.log(1.0), math.log(12.0))), 1.0, 12.0)
    slab_spectra = scatter_about(seeds[4], (2, 2 * NF, NX, NY), 1.0, 6.0, ((2, 32), (3, 16)), jnp.float32)
    monitor_spectra = heavy_noise(seeds[5], (NW, 2, 4, NX, NY), 1.0, 6.0, ((3, 32), (4, 16)), (4, 0, 16, 2.0), jnp.float32)
    wave_index = with_ends(jax.random.randint(seeds[6], (NW,), 0, NF), jax.random.fold_in(seeds[6], 1), 0, NF - 1).astype(jnp.int32)
    return {"electric": electric, "magnetic": magnetic, "material": material, "permittivity": permittivity, "slab_spectra": slab_spectra, "monitor_spectra": monitor_spectra, "wave_index": wave_index}


TIME_STEP = 0.5
OMEGA_LOW = 0.15
OMEGA_HIGH = 0.8

def forward_z(values):
    return jnp.concatenate([values[1:], jnp.zeros_like(values[:1])], axis=0) - values

def backward_z(values):
    return values - jnp.concatenate([jnp.zeros_like(values[:1]), values[:-1]], axis=0)

def inverse_map(material, permittivity):
    inverse = jnp.zeros(material.shape, jnp.float32)
    for category in range(permittivity.shape[0]):
        inverse = inverse + jnp.where(material == category, 1.0 / permittivity[category], 0.0)
    return inverse

def all_omegas(freq_count):
    return OMEGA_LOW + (OMEGA_HIGH - OMEGA_LOW) * jnp.arange(freq_count, dtype=jnp.float32) / (freq_count - 1)

def picked_omegas(wave_index, freq_count):
    matches = wave_index[:, None] == jnp.arange(freq_count, dtype=jnp.int32)[None, :]
    return lax.optimization_barrier(jnp.sum(jnp.where(matches, all_omegas(freq_count)[None, :], 0.0), axis=1))

def order_table(length, kept_count, offset, modulus):
    position = jnp.arange(length, dtype=jnp.int32) + offset
    wanted = (jnp.arange(kept_count, dtype=jnp.int32) - kept_count // 2) % modulus
    phases = position[:, None] * wanted[None, :] % modulus
    angles = 2.0 * math.pi / modulus * phases.astype(jnp.float32)
    cosine = jnp.cos(angles)
    sine_part = jnp.sin(angles)
    return jnp.stack([jnp.stack([cosine, -sine_part]), jnp.stack([sine_part, cosine])])

def advance(electric, magnetic, inverse):
    electric_x, electric_y, electric_z = (electric[0], electric[1], electric[2])
    ey_ahead_x = jnp.roll(electric_y, -1, axis=1)
    ez_ahead_x = jnp.roll(electric_z, -1, axis=1)
    ex_ahead_y = jnp.roll(electric_x, -1, axis=2)
    ez_ahead_y = jnp.roll(electric_z, -1, axis=2)
    magnetic_x = magnetic[0] - TIME_STEP * (ez_ahead_y - electric_z - forward_z(electric_y))
    magnetic_y = magnetic[1] - TIME_STEP * (forward_z(electric_x) - (ez_ahead_x - electric_z))
    magnetic_z = magnetic[2] - TIME_STEP * (ey_ahead_x - electric_y - (ex_ahead_y - electric_x))
    hy_behind_x = jnp.roll(magnetic_y, 1, axis=1)
    hz_behind_x = jnp.roll(magnetic_z, 1, axis=1)
    hx_behind_y = jnp.roll(magnetic_x, 1, axis=2)
    hz_behind_y = jnp.roll(magnetic_z, 1, axis=2)
    new_x = electric_x + TIME_STEP * inverse * (magnetic_z - hz_behind_y - backward_z(magnetic_y))
    new_y = electric_y + TIME_STEP * inverse * (backward_z(magnetic_x) - (magnetic_z - hz_behind_x))
    new_z = electric_z + TIME_STEP * inverse * (magnetic_y - hy_behind_x - (magnetic_x - hx_behind_y))
    return (jnp.stack([new_x, new_y, new_z]), jnp.stack([magnetic_x, magnetic_y, magnetic_z]))

def records_of(electric, magnetic):
    middle = electric.shape[1] // 2
    slab_layer = electric[0:2, middle]
    monitor_plane = jnp.concatenate([electric[0:2, -1], magnetic[0:2, -1]], axis=0)
    return (slab_layer, monitor_plane)

def spectra_update(slab_spectra, monitor_spectra, slab_records, monitor_records, wave_index):
    freq_count = slab_spectra.shape[1] // 2
    times = TIME_STEP * (jnp.arange(2, dtype=jnp.float32) + 1.0)
    slab_angles = times[:, None] * all_omegas(freq_count)[None, :]
    slab_table = jnp.concatenate([TIME_STEP * jnp.cos(slab_angles), -TIME_STEP * jnp.sin(slab_angles)], axis=1)
    slab_next = slab_spectra + jnp.einsum('csxy,sf->cfxy', slab_records, slab_table, precision=lax.Precision.HIGHEST)
    half_lag = jnp.array([0.0, 0.0, 0.5, 0.5], jnp.float32) * TIME_STEP
    monitor_times = times[None, :] - half_lag[:, None]
    monitor_angles = monitor_times[:, :, None] * picked_omegas(wave_index, freq_count)[None, None, :]
    real_part = jnp.einsum('csxy,csw->wcxy', monitor_records, TIME_STEP * jnp.cos(monitor_angles), precision=lax.Precision.HIGHEST)
    imag_part = jnp.einsum('csxy,csw->wcxy', monitor_records, -TIME_STEP * jnp.sin(monitor_angles), precision=lax.Precision.HIGHEST)
    monitor_next = monitor_spectra + jnp.stack([real_part, imag_part], axis=1)
    return (slab_next, monitor_next)

def reference(electric, magnetic, material, permittivity, slab_spectra, monitor_spectra, wave_index):
    inverse = inverse_map(material, permittivity)
    slab_list = []
    plane_list = []
    for repeat in range(2):
        electric, magnetic = advance(electric, magnetic, inverse)
        slab_layer, monitor_plane = records_of(electric, magnetic)
        slab_list.append(slab_layer)
        plane_list.append(monitor_plane)
    slab_records = jnp.stack(slab_list, axis=1)
    monitor_records = jnp.stack(plane_list, axis=1)
    slab_next, monitor_next = spectra_update(slab_spectra, monitor_spectra, slab_records, monitor_records, wave_index)
    y_table = order_table(NY, OY, 0, NY)
    spectrum_y = jnp.einsum('wicxy,ioyk->wockx', monitor_next, y_table, precision=lax.Precision.HIGHEST)
    x_table = order_table(NX, OX, 0, NX)
    scaling = 1.0 / math.sqrt(NX * NY)
    orders = jnp.einsum('wicqx,ioxk->wocqk', spectrum_y, x_table, precision=lax.Precision.HIGHEST) * scaling
    return (electric, magnetic, slab_next, monitor_next, orders)
```

```python
import functools
import math

import jax
import jax.numpy as jnp
import numpy as np
from jax import lax
from jax.experimental import pallas as pl
from jax.experimental.pallas import tpu as pltpu
from jax.sharding import PartitionSpec as P

MESH = pl.DeviceIdType.MESH
OX = 64
TIME_STEP = 0.5
OMEGA_LOW = 0.15
OMEGA_HIGH = 0.8
EDGE_MOVES = ((0, -1), (0, 1), (-1, -1), (1, -1), (-1, 1), (1, 1))


def omegas(freq_count):
    low, high = np.float32(OMEGA_LOW), np.float32(OMEGA_HIGH - OMEGA_LOW)
    return low + high * np.arange(freq_count, dtype=np.float32) / np.float32(freq_count - 1)


def slab_weights(freq_count):
    rows = []
    for step in (1, 2):
        angle = (np.float32(TIME_STEP * step) * omegas(freq_count)).astype(np.float64)
        rows.append(np.concatenate([TIME_STEP * np.cos(angle), -TIME_STEP * np.sin(angle)]))
    return np.stack(rows).astype(np.float32)


def monitor_weights(freq_count):
    rows = []
    for step in (1, 2):
        for lag in (0.0, 0.5):
            angle = (np.float32(TIME_STEP * (step - lag)) * omegas(freq_count)).astype(np.float64)
            rows += [TIME_STEP * np.cos(angle), -TIME_STEP * np.sin(angle)]
    return np.stack(rows).astype(np.float32)


def y_tables(gy_count, local_y, order_count):
    length = gy_count * local_y
    orders = np.arange(order_count) - order_count // 2
    inside = 2.0 * np.pi / length * (np.arange(local_y)[:, None] * orders[None, :] % length)
    blocks = 2.0 * np.pi / length * (local_y * np.arange(gy_count)[:, None] * orders[None, :] % length)
    local = np.concatenate([np.cos(inside), np.sin(inside)], axis=1)
    turn = np.stack([np.cos(blocks), np.sin(blocks)], axis=1)
    return local.astype(np.float32), turn.astype(np.float32)


def x_tables(gx_count, local_x, kept, components, full_length):
    length = gx_count * local_x
    orders = np.arange(OX) - OX // 2
    inside = 2.0 * np.pi / length * (np.arange(local_x)[:, None] * orders[None, :] % length)
    blocks = 2.0 * np.pi / length * (local_x * np.arange(gx_count)[:, None] * orders[None, :] % length)
    scale = 1.0 / math.sqrt(length * full_length)
    cosine, sine = np.cos(inside) * scale, np.sin(inside) * scale
    half = components * local_x
    local = np.zeros((128, 2 * components * OX))
    for c in range(components):
        row, column = c * local_x, c * OX
        local[row : row + local_x, column : column + OX] = cosine
        local[row : row + local_x, components * OX + column : components * OX + column + OX] = -sine
        local[half + row : half + row + local_x, column : column + OX] = sine
        local[
            half + row : half + row + local_x, components * OX + column : components * OX + column + OX
        ] = cosine
    turn = np.stack([np.cos(blocks), np.sin(blocks)])
    turn = np.repeat(turn, kept, axis=1)
    turn = np.tile(turn, (1, 1, components))
    return local.astype(np.float32), turn.astype(np.float32)


def whole_kernel(
    gx_count,
    gy_count,
    electric,
    magnetic,
    material,
    monitor,
    permittivity,
    wave_index,
    weights,
    y_local,
    y_turn,
    x_local,
    x_turn,
    electric_out,
    magnetic_out,
    monitor_out,
    slab_records,
    orders_out,
    field,
    classes,
    mbuf,
    rbuf,
    edges,
    edges_in,
    kbuf,
    kin,
    xbuf,
    records,
    load_sem,
    store_sem,
    strip_send,
    strip_recv,
    edge_send,
    edge_recv,
    a_send,
    a_recv,
    b_send,
    b_recv,
):
    gx = lax.axis_index("gx")
    gy = lax.axis_index("gy")
    kept = kbuf.shape[1]
    order_count = gx_count * kept

    def along_gx(step):
        return lax.rem(gx + (step + gx_count), gx_count)

    def along_gy(step):
        return lax.rem(gy + (step + gy_count), gy_count)

    loads = [
        pltpu.make_async_copy(electric, field.at[0:3, 1:17, 0:8, 0:128], load_sem.at[0]),
        pltpu.make_async_copy(magnetic, field.at[3:6, 1:17, 0:8, 0:128], load_sem.at[1]),
        pltpu.make_async_copy(material, classes, load_sem.at[2]),
        pltpu.make_async_copy(monitor, mbuf, load_sem.at[3]),
    ]
    for load in loads:
        load.start()

    barrier = pltpu.get_barrier_semaphore()

    def greet_x(step, carry):
        pl.semaphore_signal(barrier, inc=1, device_id=(along_gx(step), gy), device_id_type=MESH)
        return carry

    def greet_y(step, carry):
        pl.semaphore_signal(barrier, inc=1, device_id=(gx, along_gy(step)), device_id_type=MESH)
        return carry

    lax.fori_loop(1, gx_count, greet_x, 0)
    lax.fori_loop(1, gy_count, greet_y, 0)
    for dx, dy in EDGE_MOVES[2:]:
        pl.semaphore_signal(
            barrier, inc=1, device_id=(along_gx(dx), along_gy(dy)), device_id_type=MESH
        )

    field[0:6, 0] = jnp.zeros((6, 16, 256), jnp.float32)
    field[0:6, 17] = jnp.zeros((6, 16, 256), jnp.float32)

    loads[2].wait()
    inverses = [1.0 / jnp.full((8, 128), permittivity[i], jnp.float32) for i in range(4)]

    def invert(z, carry):
        here = classes[z]
        value = jnp.zeros((8, 128), jnp.float32)
        for i in range(4):
            value = value + jnp.where(here == i, inverses[i], 0.0)
        field[6, z + 1, 0:8, 0:128] = value
        return carry

    lax.fori_loop(0, 16, invert, 0)
    loads[0].wait()
    loads[1].wait()

    lane = lax.broadcasted_iota(jnp.int32, (8, 128), 1)
    sublane = lax.broadcasted_iota(jnp.int32, (8, 128), 0)

    def tile_of(v, k):
        return 2 * v + k // 16, lax.rem(k, 16) + 1

    def pack(k, held):
        mask = lane // 4 == k
        new = []
        for v in range(4):
            if v < 3:
                c, z = tile_of(v, k)
                tile = field[c, z, 0:8, 0:128]
            else:
                tile = field[6, lax.rem(k, 16) + 1, 0:8, 0:128]
            new.append(jnp.where(mask, pltpu.roll(tile, lax.rem(4 * k + 2, 128), 1), held[v]))
        return tuple(new)

    packed = lax.fori_loop(0, 32, pack, tuple(jnp.zeros((8, 128), jnp.float32) for _ in range(4)))
    for v in range(4):
        edges[v] = packed[v]

    pl.semaphore_wait(barrier, gx_count - 1 + gy_count - 1 + 4)

    strips = []
    for i, (step, first, landing) in enumerate(((-1, 0, 8), (1, 6, 14))):
        strips.append(
            pltpu.make_async_remote_copy(
                src_ref=field.at[:, 1:17, first : first + 2, 0:128],
                dst_ref=field.at[:, 1:17, landing : landing + 2, 0:128],
                send_sem=strip_send.at[i],
                recv_sem=strip_recv.at[i],
                device_id=(along_gx(step), gy),
                device_id_type=MESH,
            )
        )
    shares = []
    for i, (dx, dy) in enumerate(EDGE_MOVES):
        shares.append(
            pltpu.make_async_remote_copy(
                src_ref=edges,
                dst_ref=edges_in.at[i],
                send_sem=edge_send.at[i],
                recv_sem=edge_recv.at[i],
                device_id=(along_gx(dx), along_gy(dy)),
                device_id_type=MESH,
            )
        )
    for copy in shares[2:] + shares[:2] + strips:
        copy.start()
    for copy in shares:
        copy.wait_recv()

    ahead = lax.rem(lane, 4) >= 2
    top = sublane < 4
    side, corner = [], []
    for v in range(4):
        side.append(jnp.where(ahead, edges_in[0, v], edges_in[1, v]))
        corner.append(
            jnp.where(
                ahead,
                jnp.where(top, edges_in[2, v], edges_in[3, v]),
                jnp.where(top, edges_in[4, v], edges_in[5, v]),
            )
        )

    def unpack(k, carry):
        shift = lax.rem(126 - 4 * k + 128, 128)
        for v in range(4):
            if v < 3:
                c, z = tile_of(v, k)
            else:
                c, z = 6, lax.rem(k, 16) + 1
            field[c, z, 0:8, 128:256] = pltpu.roll(side[v], shift, 1)
            field[c, z, 8:16, 128:256] = pltpu.roll(corner[v], shift, 1)
        return carry

    lax.fori_loop(0, 32, unpack, 0)
    for copy in strips:
        copy.wait()

    def x_ahead(value):
        return pltpu.roll(value, 15, 0)

    def x_behind(value):
        return pltpu.roll(value, 1, 0)

    def y_ahead(value):
        return pltpu.roll(value, 255, 1)

    def y_behind(value):
        return pltpu.roll(value, 1, 1)

    def step_h(z, carry):
        ex, ey, ez = field[0, z], field[1, z], field[2, z]
        ex_up, ey_up = field[0, z + 1], field[1, z + 1]
        field[3, z] = field[3, z] - TIME_STEP * (y_ahead(ez) - ez - (ey_up - ey))
        field[4, z] = field[4, z] - TIME_STEP * ((ex_up - ex) - (x_ahead(ez) - ez))
        field[5, z] = field[5, z] - TIME_STEP * (x_ahead(ey) - ey - (y_ahead(ex) - ex))
        return carry

    def step_e(z, carry):
        hx, hy, hz = field[3, z], field[4, z], field[5, z]
        hx_down, hy_down = field[3, z - 1], field[4, z - 1]
        rate = TIME_STEP * field[6, z]
        field[0, z] = field[0, z] + rate * (hz - y_behind(hz) - (hy - hy_down))
        field[1, z] = field[1, z] + rate * ((hx - hx_down) - (hz - x_behind(hz)))
        field[2, z] = field[2, z] + rate * (hy - x_behind(hy) - (hx - y_behind(hx)))
        return carry

    for step in range(2):
        lax.fori_loop(1, 17, step_h, 0)
        lax.fori_loop(1, 17, step_e, 0)
        for c in range(2):
            slab_records[c, step] = field[c, 9, 0:8, 0:128]
        for c, row in enumerate((0, 1, 3, 4)):
            records[step, c] = field[row, 16, 0:8, 0:128]

    stores = [
        pltpu.make_async_copy(field.at[0:3, 1:17, 0:8, 0:128], electric_out, store_sem.at[0]),
        pltpu.make_async_copy(field.at[3:6, 1:17, 0:8, 0:128], magnetic_out, store_sem.at[1]),
    ]
    loads[3].wait()

    def a_copy(w, b, slot):
        return pltpu.make_async_remote_copy(
            src_ref=mbuf.at[w],
            dst_ref=rbuf.at[b],
            send_sem=a_send.at[slot],
            recv_sem=a_recv.at[b],
            device_id=(gx, w),
            device_id_type=MESH,
        )

    half = gy_count // 2
    far_first = [half]
    for i in range(1, half):
        far_first += [half - i, half + i]
    for step in far_first + [0]:
        w = along_gy(step)
        pick = wave_index[w]
        for i in range(2):
            for c in range(4):
                value = mbuf[w, 4 * i + c]
                for s in range(2):
                    value = value + weights[4 * s + 2 * (c // 2) + i, pick] * records[s, c]
                mbuf[w, 4 * i + c] = value
        if step:
            a_copy(w, gy, step).start()
    for store in stores:
        store.start()
    monitor_store = pltpu.make_async_copy(mbuf, monitor_out, store_sem.at[2])
    monitor_store.start()

    def y_part(data, b, real, imag):
        rows = data.reshape(64, 128)
        product = jnp.dot(
            rows, y_local[...], precision=lax.Precision.HIGHEST, preferred_element_type=jnp.float32
        )
        a_cos, a_sin = product[0:32, 0:order_count], product[0:32, order_count:]
        b_cos, b_sin = product[32:64, 0:order_count], product[32:64, order_count:]
        re, im = a_cos + b_sin, b_cos - a_sin
        turn = y_turn[b]
        cosine, sine = turn[0:1, :], turn[1:2, :]
        return real + (re * cosine + im * sine), imag + (im * cosine - re * sine)

    real = jnp.zeros((32, order_count), jnp.float32)
    real, imag = y_part(mbuf[gy], gy, real, real)
    for step in far_first[::-1]:
        b = along_gy(-step)
        a_copy(along_gy(step), b, step).wait_recv()
        real, imag = y_part(rbuf[b], b, real, imag)

    spectrum = jnp.concatenate([real, imag, jnp.zeros((64, order_count), jnp.float32)], axis=0)
    turned = jnp.transpose(spectrum)
    for g in range(gx_count):
        kbuf[g] = turned[kept * g : kept * (g + 1), :]

    def b_copy(g, own, slot):
        return pltpu.make_async_remote_copy(
            src_ref=kbuf.at[g],
            dst_ref=kin.at[own],
            send_sem=b_send.at[slot],
            recv_sem=b_recv.at[own],
            device_id=(g, gy),
            device_id_type=MESH,
        )

    def send_b(step, carry):
        b_copy(along_gx(step), gx, step).start()
        return carry

    def take_b(step, carry):
        b_copy(along_gx(step), along_gx(-step), step).wait_recv()
        return carry

    lax.fori_loop(1, gx_count, send_b, 0)
    kin[gx] = kbuf[gx]
    lax.fori_loop(1, gx_count, take_b, 0)
    for g in range(gx_count):
        xbuf[kept * g : kept * (g + 1), :] = kin[g]
    product = jnp.dot(
        xbuf[...], x_local[...], precision=lax.Precision.HIGHEST, preferred_element_type=jnp.float32
    )
    width = 4 * OX
    re, im = product[:, 0:width], product[:, width:]
    cosine, sine = x_turn[0], x_turn[1]
    out_re = re * cosine + im * sine
    out_im = im * cosine - re * sine
    for part, value in enumerate((out_re, out_im)):
        total = value[0:8]
        for r in range(8, kept * gx_count, 8):
            total = total + value[r : r + 8]
        total = total[0:kept] + total[kept : 2 * kept]
        for c in range(4):
            orders_out[0, part, c] = total[:, c * OX : (c + 1) * OX]

    for copy in shares:
        copy.wait_send()

    def sent_a(step, carry):
        a_copy(along_gy(step), gy, step).wait_send()
        return carry

    def sent_b(step, carry):
        b_copy(along_gx(step), gx, step).wait_send()
        return carry

    lax.fori_loop(1, gy_count, sent_a, 0)
    lax.fori_loop(1, gx_count, sent_b, 0)
    for store in stores:
        store.wait()
    monitor_store.wait()


def per_device(
    gx_count,
    gy_count,
    order_count,
    electric,
    magnetic,
    material,
    permittivity,
    slab_spectra,
    monitor_spectra,
    wave_index,
):
    freq_count = slab_spectra.shape[1] // 2
    kept = order_count // gx_count
    y_local, y_turn = y_tables(gy_count, 128, order_count)
    x_local, x_turn = x_tables(gx_count, 8, kept, 4, gy_count * 128)
    monitor_flat = monitor_spectra.reshape(gy_count, 8, 8, 128)
    hbm = pl.BlockSpec(memory_space=pl.ANY)
    vmem = pl.BlockSpec(memory_space=pltpu.VMEM)
    smem = pl.BlockSpec(memory_space=pltpu.SMEM)
    f32 = jnp.float32
    dma = pltpu.SemaphoreType.DMA
    electric_next, magnetic_next, monitor_next, slab_records, orders = pl.pallas_call(
        functools.partial(whole_kernel, gx_count, gy_count),
        name="leapfrog_orders",
        out_shape=(
            jax.ShapeDtypeStruct(electric.shape, f32),
            jax.ShapeDtypeStruct(magnetic.shape, f32),
            jax.ShapeDtypeStruct(monitor_flat.shape, f32),
            jax.ShapeDtypeStruct((2, 2, 8, 128), f32),
            jax.ShapeDtypeStruct((1, 2, 4, kept, OX), f32),
        ),
        in_specs=[hbm] * 4 + [smem] * 3 + [vmem] * 4,
        out_specs=(hbm, hbm, hbm, vmem, vmem),
        scratch_shapes=[
            pltpu.VMEM((7, 18, 16, 256), f32),
            pltpu.VMEM((16, 8, 128), jnp.int32),
            pltpu.VMEM((gy_count, 8, 8, 128), f32),
            pltpu.VMEM((gy_count, 8, 8, 128), f32),
            pltpu.VMEM((4, 8, 128), f32),
            pltpu.VMEM((6, 4, 8, 128), f32),
            pltpu.VMEM((gx_count, kept, 128), f32),
            pltpu.VMEM((gx_count, kept, 128), f32),
            pltpu.VMEM((gx_count * kept, 128), f32),
            pltpu.VMEM((2, 4, 8, 128), f32),
            dma((4,)),
            dma((3,)),
            dma((2,)),
            dma((2,)),
            dma((6,)),
            dma((6,)),
            dma((gy_count,)),
            dma((gy_count,)),
            dma((gx_count,)),
            dma((gx_count,)),
        ],
        compiler_params=pltpu.CompilerParams(collective_id=0, has_side_effects=True),
    )(
        electric,
        magnetic,
        material,
        monitor_flat,
        permittivity,
        wave_index,
        jnp.asarray(monitor_weights(freq_count)),
        jnp.asarray(y_local),
        jnp.asarray(y_turn),
        jnp.asarray(x_local),
        jnp.asarray(x_turn),
    )
    table = jnp.asarray(slab_weights(freq_count))
    slab_next = slab_spectra + (
        table[0][None, :, None, None] * slab_records[:, 0][:, None]
        + table[1][None, :, None, None] * slab_records[:, 1][:, None]
    )
    return (
        electric_next,
        magnetic_next,
        slab_next,
        monitor_next.reshape(monitor_spectra.shape),
        orders,
    )


def solution(mesh, order_count=128):
    fields = P(None, None, "gx", "gy")
    spectra = P(None, None, None, "gx", "gy")
    return jax.shard_map(
        functools.partial(per_device, mesh.shape["gx"], mesh.shape["gy"], order_count),
        mesh=mesh,
        in_specs=(fields, fields, P(None, "gx", "gy"), P(), fields, spectra, P()),
        out_specs=(fields, fields, fields, spectra, P("gy", None, None, "gx", None)),
        check_vma=False,
    )
```

```python
import functools
import math

import jax
import jax.numpy as jnp
import numpy as np
from jax import lax
from jax.experimental import pallas as pl
from jax.experimental.pallas import tpu as pltpu
from jax.sharding import PartitionSpec as P

MESH = pl.DeviceIdType.MESH
OX = 64
TIME_STEP = 0.5
OMEGA_LOW = 0.15
OMEGA_HIGH = 0.8
EDGE_MOVES = ((0, -1), (0, 1), (-1, 0), (1, 0), (-1, -1), (1, -1), (-1, 1), (1, 1))


def omegas(freq_count):
    low, high = np.float32(OMEGA_LOW), np.float32(OMEGA_HIGH - OMEGA_LOW)
    return low + high * np.arange(freq_count, dtype=np.float32) / np.float32(freq_count - 1)


def slab_weights(freq_count):
    rows = []
    for step in (1, 2):
        angle = (np.float32(TIME_STEP * step) * omegas(freq_count)).astype(np.float64)
        rows.append(np.concatenate([TIME_STEP * np.cos(angle), -TIME_STEP * np.sin(angle)]))
    return np.stack(rows).astype(np.float32)


def monitor_weights(freq_count):
    rows = []
    for step in (1, 2):
        for lag in (0.0, 0.5):
            angle = (np.float32(TIME_STEP * (step - lag)) * omegas(freq_count)).astype(np.float64)
            rows += [TIME_STEP * np.cos(angle), -TIME_STEP * np.sin(angle)]
    return np.stack(rows).astype(np.float32)


def split_table(table):
    table = table.astype(np.float32)
    lead = table.astype(jnp.bfloat16)
    rest = (table - lead.astype(np.float32)).astype(jnp.bfloat16)
    return np.concatenate([lead, lead], axis=0), rest


def y_tables(gy_count, local_y, order_count):
    length = gy_count * local_y
    orders = np.arange(order_count) - order_count // 2
    inside = 2.0 * np.pi / length * (np.arange(local_y)[:, None] * orders[None, :] % length)
    blocks = 2.0 * np.pi / length * (local_y * np.arange(gy_count)[:, None] * orders[None, :] % length)
    local = np.concatenate([np.cos(inside), np.sin(inside)], axis=1)
    turn = np.stack([np.cos(blocks), np.sin(blocks)], axis=1)
    return split_table(local), turn.astype(np.float32)


def x_local_table(gx_count, local_x, components, full_length):
    length = gx_count * local_x
    orders = np.arange(OX) - OX // 2
    inside = 2.0 * np.pi / length * (np.arange(local_x)[:, None] * orders[None, :] % length)
    scale = 1.0 / math.sqrt(length * full_length)
    cosine, sine = np.cos(inside) * scale, np.sin(inside) * scale
    half, wide = components * local_x, components * OX
    local = np.zeros((128, 2 * wide))
    for c in range(components):
        real = slice(c * local_x, (c + 1) * local_x)
        imag = slice(half + c * local_x, half + (c + 1) * local_x)
        to_real = slice(c * OX, (c + 1) * OX)
        to_imag = slice(wide + c * OX, wide + (c + 1) * OX)
        local[real, to_real], local[real, to_imag] = cosine, -sine
        local[imag, to_real], local[imag, to_imag] = sine, cosine
    return split_table(local)


def x_turn_table(gx_count, local_x, kept):
    length = gx_count * local_x
    orders = np.arange(OX) - OX // 2
    blocks = 2.0 * np.pi / length * (local_x * np.arange(gx_count)[:, None] * orders[None, :] % length)
    turn = np.repeat(np.stack([np.cos(blocks), np.sin(blocks)]), kept, axis=1)
    return np.tile(turn, (1, 1, 2)).astype(np.float32)


def split_dot(value, table, rest):
    lead = value.astype(jnp.bfloat16)
    low = (value - lead.astype(jnp.float32)).astype(jnp.bfloat16)
    return jnp.dot(
        jnp.concatenate([lead, low], axis=1), table, preferred_element_type=jnp.float32
    ) + jnp.dot(lead, rest, preferred_element_type=jnp.float32)


def whole_kernel(
    gx_count,
    gy_count,
    electric,
    magnetic,
    material,
    monitor,
    slab,
    y_lead_in,
    y_rest_in,
    y_turn_in,
    xm_lead_in,
    xm_rest_in,
    xf_lead_in,
    xf_rest_in,
    x_turn_in,
    permittivity,
    wave_index,
    weights,
    slab_table,
    electric_out,
    magnetic_out,
    slab_out,
    monitor_out,
    orders_out,
    field,
    strip,
    classes,
    mbuf,
    rbuf,
    edges,
    edges_in,
    kbuf_m,
    kin_m,
    kbuf_f,
    kin_f,
    xbuf,
    share,
    share_in,
    records,
    slab_records,
    y_lead,
    y_rest,
    y_turn,
    xm_lead,
    xm_rest,
    xf_lead,
    xf_rest,
    x_turn,
    load_sem,
    strip_send,
    strip_recv,
    edge_send,
    edge_recv,
    a_send,
    a_recv,
    m_send,
    m_recv,
    f_send,
    f_recv,
    c_send,
    c_recv,
):
    gx = lax.axis_index("gx")
    gy = lax.axis_index("gy")
    kept = kbuf_m.shape[1]
    order_count = gx_count * kept

    def along_gx(step):
        return lax.rem(gx + (step + gx_count), gx_count)

    def along_gy(step):
        return lax.rem(gy + (step + gy_count), gy_count)

    loads = [
        pltpu.make_async_copy(source, target, load_sem.at[i])
        for i, (source, target) in enumerate(
            (
                (material, classes),
                (electric, field.at[0:3, 1:17, 0:8, :]),
                (magnetic, field.at[3:6, 1:17, 0:8, :]),
                (monitor, mbuf),
                (slab, slab_out),
                (y_lead_in, y_lead),
                (y_rest_in, y_rest),
                (y_turn_in, y_turn),
                (xm_lead_in, xm_lead),
                (xm_rest_in, xm_rest),
                (xf_lead_in, xf_lead),
                (xf_rest_in, xf_rest),
                (x_turn_in, x_turn),
            )
        )
    ]
    for load in loads:
        load.start()

    barrier = pltpu.get_barrier_semaphore()

    def greet_x(step, carry):
        pl.semaphore_signal(barrier, inc=1, device_id=(along_gx(step), gy), device_id_type=MESH)
        return carry

    def greet_y(step, carry):
        pl.semaphore_signal(barrier, inc=1, device_id=(gx, along_gy(step)), device_id_type=MESH)
        return carry

    lax.fori_loop(1, gx_count, greet_x, 0)
    lax.fori_loop(1, gy_count, greet_y, 0)
    for dx, dy in EDGE_MOVES[4:]:
        pl.semaphore_signal(
            barrier, inc=1, device_id=(along_gx(dx), along_gy(dy)), device_id_type=MESH
        )

    field[0:6, 0] = jnp.zeros((6, 16, 128), jnp.float32)
    field[0:6, 17] = jnp.zeros((6, 16, 128), jnp.float32)

    loads[0].wait()
    inverses = [1.0 / jnp.full((8, 128), permittivity[i], jnp.float32) for i in range(4)]
    for z in range(16):
        here = classes[z]
        value = jnp.zeros((8, 128), jnp.float32)
        for i in range(4):
            value = value + jnp.where(here == i, inverses[i], 0.0)
        field[6, z + 1, 0:8, :] = value
    loads[1].wait()
    loads[2].wait()

    lane = lax.broadcasted_iota(jnp.int32, (8, 128), 1)
    top = lax.broadcasted_iota(jnp.int32, (8, 128), 0) < 4
    cell = lax.rem(lane, 8)

    def pack(c, carry):
        held = jnp.zeros((8, 128), jnp.float32)
        for z in range(16):
            tile = field[c, z + 1, 0:8, :]
            held = jnp.where(lane // 8 == z, pltpu.roll(tile, (8 * z + 2) % 128, 1), held)
        edges[c] = held
        return carry

    lax.fori_loop(0, 7, pack, 0)
    loads[3].wait()

    pl.semaphore_wait(barrier, gx_count - 1 + gy_count - 1 + 4)

    shares = []
    for i, (dx, dy) in enumerate(EDGE_MOVES):
        shares.append(
            pltpu.make_async_remote_copy(
                src_ref=edges,
                dst_ref=edges_in.at[i],
                send_sem=edge_send.at[i],
                recv_sem=edge_recv.at[i],
                device_id=(along_gx(dx), along_gy(dy)),
                device_id_type=MESH,
            )
        )
    strips = []
    for i, (step, first, landing) in enumerate(((-1, 0, 8), (1, 6, 14))):
        strips.append(
            pltpu.make_async_remote_copy(
                src_ref=field.at[:, 1:17, first : first + 2, :],
                dst_ref=field.at[:, 1:17, landing : landing + 2, :],
                send_sem=strip_send.at[i],
                recv_sem=strip_recv.at[i],
                device_id=(along_gx(step), gy),
                device_id_type=MESH,
            )
        )
    for copy in shares[::-1] + strips:
        copy.start()

    def a_copy(w, b, slot):
        return pltpu.make_async_remote_copy(
            src_ref=mbuf.at[w],
            dst_ref=rbuf.at[b],
            send_sem=a_send.at[slot],
            recv_sem=a_recv.at[b],
            device_id=(gx, w),
            device_id_type=MESH,
        )

    half = gy_count // 2
    far_first = [half]
    for i in range(1, half):
        far_first += [half - i, half + i]
    for step in far_first:
        a_copy(along_gy(step), gy, step).start()
    for copy in shares:
        copy.wait_recv()

    def edge_strip(me, ahead, behind):
        low = jnp.where(cell < 2, behind, me)
        high = pltpu.roll(jnp.where(cell < 2, me, ahead), 4, 1)
        return jnp.where(cell < 4, low, high)

    for c in range(7):
        strip[c, 0:8] = edge_strip(edges[c], edges_in[0, c], edges_in[1, c])
        strip[c, 8:16] = edge_strip(
            jnp.where(top, edges_in[2, c], edges_in[3, c]),
            jnp.where(top, edges_in[4, c], edges_in[5, c]),
            jnp.where(top, edges_in[6, c], edges_in[7, c]),
        )
    for copy in strips:
        copy.wait()

    wide_lane = lax.broadcasted_iota(jnp.int32, (16, 128), 1)
    last_lane, first_lane = wide_lane == 127, wide_lane == 0
    last_layer, first_layer = wide_lane >= 120, wide_lane < 8

    def x_ahead(value):
        return pltpu.roll(value, 15, 0)

    def x_behind(value):
        return pltpu.roll(value, 1, 0)

    def strip_h():
        ex, ey, ez = strip[0], strip[1], strip[2]
        ex_up = jnp.where(last_layer, 0.0, pltpu.roll(ex, 120, 1))
        ey_up = jnp.where(last_layer, 0.0, pltpu.roll(ey, 120, 1))
        ez_y, ex_y = pltpu.roll(ez, 127, 1), pltpu.roll(ex, 127, 1)
        strip[3] = strip[3] - TIME_STEP * (ez_y - ez - (ey_up - ey))
        strip[4] = strip[4] - TIME_STEP * ((ex_up - ex) - (x_ahead(ez) - ez))
        strip[5] = strip[5] - TIME_STEP * (x_ahead(ey) - ey - (ex_y - ex))

    def strip_e():
        hx, hy, hz = strip[3], strip[4], strip[5]
        hx_down = jnp.where(first_layer, 0.0, pltpu.roll(hx, 8, 1))
        hy_down = jnp.where(first_layer, 0.0, pltpu.roll(hy, 8, 1))
        hz_y, hx_y = pltpu.roll(hz, 1, 1), pltpu.roll(hx, 1, 1)
        rate = TIME_STEP * strip[6]
        strip[0] = strip[0] + rate * (hz - hz_y - (hy - hy_down))
        strip[1] = strip[1] + rate * ((hx - hx_down) - (hz - x_behind(hz)))
        strip[2] = strip[2] + rate * (hy - x_behind(hy) - (hx - hx_y))

    def main_h(z):
        def y_ahead(value, c):
            edge = pltpu.roll(strip[c], (129 - 8 * z), 1)
            return jnp.where(last_lane, edge, pltpu.roll(value, 127, 1))

        ex, ey, ez = field[0, z], field[1, z], field[2, z]
        ex_up, ey_up = field[0, z + 1], field[1, z + 1]
        field[3, z] = field[3, z] - TIME_STEP * (y_ahead(ez, 2) - ez - (ey_up - ey))
        field[4, z] = field[4, z] - TIME_STEP * ((ex_up - ex) - (x_ahead(ez) - ez))
        field[5, z] = field[5, z] - TIME_STEP * (x_ahead(ey) - ey - (y_ahead(ex, 0) - ex))

    def main_e(z):
        def y_behind(value, c):
            edge = pltpu.roll(strip[c], (135 - 8 * z) % 128, 1)
            return jnp.where(first_lane, edge, pltpu.roll(value, 1, 1))

        hx, hy, hz = field[3, z], field[4, z], field[5, z]
        hx_down, hy_down = field[3, z - 1], field[4, z - 1]
        rate = TIME_STEP * field[6, z]
        field[0, z] = field[0, z] + rate * (hz - y_behind(hz, 5) - (hy - hy_down))
        field[1, z] = field[1, z] + rate * ((hx - hx_down) - (hz - x_behind(hz)))
        field[2, z] = field[2, z] + rate * (hy - x_behind(hy) - (hx - y_behind(hx, 3)))

    def one_step(step, carry):
        for z in range(1, 17):
            main_h(z)
        strip_h()
        for z in range(1, 17):
            main_e(z)
        strip_e()
        for c in range(2):
            slab_records[c, step] = field[c, 9, 0:8, :]
        for c, row in enumerate((0, 1, 3, 4)):
            records[step, c] = field[row, 16, 0:8, :]
        return carry

    lax.fori_loop(0, 2, one_step, 0)

    for load in loads[5:]:
        load.wait()

    def own_turn(re, im, b):
        turn = y_turn[b]
        cosine, sine = turn[0:1, :], turn[1:2, :]
        return re * cosine + im * sine, im * cosine - re * sine

    product = split_dot(records[...].reshape(64, 128), y_lead[...], y_rest[...])
    re, im = own_turn(product[:, 0:order_count], -product[:, order_count:], gy)
    turned = jnp.transpose(jnp.concatenate([re, im], axis=0))
    for g in range(gx_count):
        kbuf_f[g] = turned[kept * g : kept * (g + 1), :]

    def x_copy(source, target, send_sem, recv_sem, g, own, slot):
        return pltpu.make_async_remote_copy(
            src_ref=source.at[g],
            dst_ref=target.at[own],
            send_sem=send_sem.at[slot],
            recv_sem=recv_sem.at[own],
            device_id=(g, gy),
            device_id_type=MESH,
        )

    def send_f(step, carry):
        x_copy(kbuf_f, kin_f, f_send, f_recv, along_gx(step), gx, step).start()
        return carry

    def take_f(step, carry):
        x_copy(
            kbuf_f, kin_f, f_send, f_recv, along_gx(step), along_gx(-step), step
        ).wait_recv()
        return carry

    def send_m(step, carry):
        x_copy(kbuf_m, kin_m, m_send, m_recv, along_gx(step), gx, step).start()
        return carry

    def take_m(step, carry):
        x_copy(
            kbuf_m, kin_m, m_send, m_recv, along_gx(step), along_gx(-step), step
        ).wait_recv()
        return carry

    lax.fori_loop(1, gx_count, send_f, 0)
    kin_f[gx] = kbuf_f[gx]

    def hand_out(z, carry):
        for c in range(3):
            electric_out[c, z] = field[c, z + 1, 0:8, :]
            magnetic_out[c, z] = field[3 + c, z + 1, 0:8, :]
        return carry

    lax.fori_loop(0, 16, hand_out, 0)
    loads[4].wait()
    slab_held = [[slab_records[c, s] for s in range(2)] for c in range(2)]

    def slab_update(i, carry):
        for j in range(4):
            f = 4 * i + j
            first, second = slab_table[0, f], slab_table[1, f]
            for c in range(2):
                slab_out[c, f] = slab_out[c, f] + (
                    first * slab_held[c][0] + second * slab_held[c][1]
                )
        return carry

    lax.fori_loop(0, slab_out.shape[1] // 4, slab_update, 0)
    held = [[records[s, c] for c in range(4)] for s in range(2)]

    def weights_of(w):
        pick = wave_index[w]
        return [
            [[weights[4 * s + 2 * kind + i, pick] for i in range(2)] for kind in range(2)]
            for s in range(2)
        ]

    def monitor_update(w, carry):
        scale = weights_of(w)
        for i in range(2):
            for c in range(4):
                monitor_out[w, 4 * i + c] = mbuf[w, 4 * i + c] + (
                    scale[0][c // 2][i] * held[0][c] + scale[1][c // 2][i] * held[1][c]
                )
        return carry

    lax.fori_loop(0, gy_count, monitor_update, 0)

    def x_sums(kin, lead, rest, blocks):
        for g in range(gx_count):
            xbuf[kept * g : kept * (g + 1), :] = kin[g]
        product = split_dot(xbuf[...], lead[...], rest[...])
        cosine, sine = x_turn[0], x_turn[1]

        def folded(value):
            total = value[0:8]
            for r in range(8, kept * gx_count, 8):
                total = total + value[r : r + 8]
            return total[0:kept] + total[kept : 2 * kept]

        real, imag = [], []
        for j in range(blocks):
            re = product[:, 128 * j : 128 * (j + 1)]
            im = product[:, 128 * (blocks + j) : 128 * (blocks + j + 1)]
            real.append(folded(re * cosine + im * sine))
            imag.append(folded(im * cosine - re * sine))
        return real, imag

    lax.fori_loop(1, gx_count, take_f, 0)
    f_real, f_imag = x_sums(kin_f, xf_lead, xf_rest, 4)

    def weigh(w, carry):
        scale = weights_of(w)
        for kind in range(2):
            (r0, i0), (r1, i1) = scale[0][kind], scale[1][kind]
            re0, im0, re1, im1 = f_real[kind], f_imag[kind], f_real[2 + kind], f_imag[2 + kind]
            share[w, :, 128 * kind : 128 * (kind + 1)] = (r0 * re0 - i0 * im0) + (r1 * re1 - i1 * im1)
            share[w, :, 128 * (2 + kind) : 128 * (3 + kind)] = (r0 * im0 + i0 * re0) + (
                r1 * im1 + i1 * re1
            )
        return carry

    lax.fori_loop(0, gy_count, weigh, 0)

    def c_copy(w, b, slot):
        return pltpu.make_async_remote_copy(
            src_ref=share.at[w],
            dst_ref=share_in.at[b],
            send_sem=c_send.at[slot],
            recv_sem=c_recv.at[b],
            device_id=(gx, w),
            device_id_type=MESH,
        )

    for step in far_first:
        c_copy(along_gy(step), gy, step).start()

    def y_part(blocks, owners, real, imag):
        rows = jnp.concatenate([block.reshape(64, 128) for block in blocks], axis=0)
        product = split_dot(rows, y_lead[...], y_rest[...])
        for i, b in enumerate(owners):
            a, c = product[64 * i : 64 * i + 32], product[64 * i + 32 : 64 * i + 64]
            re = a[:, 0:order_count] + c[:, order_count:]
            im = c[:, 0:order_count] - a[:, order_count:]
            re, im = own_turn(re, im, b)
            real, imag = real + re, imag + im
        return real, imag

    real = jnp.zeros((32, order_count), jnp.float32)
    imag = real
    arriving = [0] + far_first[::-1]
    for i in range(0, gy_count, 4):
        blocks, owners = [], []
        for step in arriving[i : i + 4]:
            b = along_gy(-step)
            if step:
                a_copy(along_gy(step), b, step).wait_recv()
                blocks.append(rbuf[b])
            else:
                blocks.append(mbuf[b])
            owners.append(b)
        real, imag = y_part(blocks, owners, real, imag)

    spectrum = jnp.concatenate([real, imag, jnp.zeros((64, order_count), jnp.float32)], axis=0)
    turned = jnp.transpose(spectrum)
    for g in range(gx_count):
        kbuf_m[g] = turned[kept * g : kept * (g + 1), :]
    lax.fori_loop(1, gx_count, send_m, 0)
    kin_m[gx] = kbuf_m[gx]

    total = share[gy]
    for step in far_first[::-1]:
        b = along_gy(-step)
        c_copy(along_gy(step), b, step).wait_recv()
        total = total + share_in[b]

    lax.fori_loop(1, gx_count, take_m, 0)
    m_real, m_imag = x_sums(kin_m, xm_lead, xm_rest, 2)
    for part, blocks in enumerate((m_real, m_imag)):
        for kind in range(2):
            first = 128 * (2 * part + kind)
            value = total[:, first : first + 128] + blocks[kind]
            for c in range(2):
                orders_out[0, part, 2 * kind + c] = value[:, c * OX : (c + 1) * OX]

    for copy in shares:
        copy.wait_send()

    def sent_y(step, carry):
        a_copy(along_gy(step), gy, step).wait_send()
        c_copy(along_gy(step), gy, step).wait_send()
        return carry

    def sent_x(step, carry):
        x_copy(kbuf_f, kin_f, f_send, f_recv, along_gx(step), gx, step).wait_send()
        x_copy(kbuf_m, kin_m, m_send, m_recv, along_gx(step), gx, step).wait_send()
        return carry

    lax.fori_loop(1, gy_count, sent_y, 0)
    lax.fori_loop(1, gx_count, sent_x, 0)


def hand_over_kernel(*refs):
    count = len(refs) // 2
    copies = [
        pltpu.make_async_copy(source, target, refs[-1].at[i])
        for i, (source, target) in enumerate(zip(refs[:count], refs[count:-1]))
    ]
    for copy in copies:
        copy.start()
    for copy in copies:
        copy.wait()


def per_device(
    gx_count,
    gy_count,
    order_count,
    electric,
    magnetic,
    material,
    permittivity,
    slab_spectra,
    monitor_spectra,
    wave_index,
):
    freq_count = slab_spectra.shape[1] // 2
    kept = order_count // gx_count
    (y_lead, y_rest), y_turn = y_tables(gy_count, 128, order_count)
    xm_lead, xm_rest = x_local_table(gx_count, 8, 4, gy_count * 128)
    xf_lead, xf_rest = x_local_table(gx_count, 8, 8, gy_count * 128)
    x_turn = x_turn_table(gx_count, 8, kept)
    tables = [y_lead, y_rest, y_turn, xm_lead, xm_rest, xf_lead, xf_rest, x_turn]
    monitor_flat = monitor_spectra.reshape(gy_count, 8, 8, 128)
    hbm = pl.BlockSpec(memory_space=pl.ANY)
    vmem = pl.BlockSpec(memory_space=pltpu.VMEM)
    smem = pl.BlockSpec(memory_space=pltpu.SMEM)
    f32 = jnp.float32
    dma = pltpu.SemaphoreType.DMA
    held = pl.pallas_call(
        functools.partial(whole_kernel, gx_count, gy_count),
        name="leapfrog_orders",
        out_shape=(
            pltpu.VMEM(electric.shape, f32),
            pltpu.VMEM(magnetic.shape, f32),
            pltpu.VMEM(slab_spectra.shape, f32),
            pltpu.VMEM(monitor_flat.shape, f32),
            pltpu.VMEM((1, 2, 4, kept, OX), f32),
        ),
        in_specs=[hbm] * 13 + [smem] * 4,
        out_specs=(vmem,) * 5,
        scratch_shapes=[
            pltpu.VMEM((7, 18, 16, 128), f32),
            pltpu.VMEM((7, 16, 128), f32),
            pltpu.VMEM((16, 8, 128), jnp.int32),
            pltpu.VMEM((gy_count, 8, 8, 128), f32),
            pltpu.VMEM((gy_count, 8, 8, 128), f32),
            pltpu.VMEM((7, 8, 128), f32),
            pltpu.VMEM((8, 7, 8, 128), f32),
            pltpu.VMEM((gx_count, kept, 128), f32),
            pltpu.VMEM((gx_count, kept, 128), f32),
            pltpu.VMEM((gx_count, kept, 128), f32),
            pltpu.VMEM((gx_count, kept, 128), f32),
            pltpu.VMEM((gx_count * kept, 128), f32),
            pltpu.VMEM((gy_count, kept, 512), f32),
            pltpu.VMEM((gy_count, kept, 512), f32),
            pltpu.VMEM((2, 4, 8, 128), f32),
            pltpu.VMEM((2, 2, 8, 128), f32),
        ]
        + [pltpu.VMEM(table.shape, table.dtype) for table in tables]
        + [
            dma((13,)),
            dma((2,)),
            dma((2,)),
            dma((8,)),
            dma((8,)),
            dma((gy_count,)),
            dma((gy_count,)),
            dma((gx_count,)),
            dma((gx_count,)),
            dma((gx_count,)),
            dma((gx_count,)),
            dma((gy_count,)),
            dma((gy_count,)),
        ],
        compiler_params=pltpu.CompilerParams(collective_id=0, has_side_effects=True),
    )(
        electric,
        magnetic,
        material,
        monitor_flat,
        slab_spectra,
        *[jnp.asarray(table) for table in tables],
        permittivity,
        wave_index,
        jnp.asarray(monitor_weights(freq_count)),
        jnp.asarray(slab_weights(freq_count)),
    )
    electric_next, magnetic_next, slab_next, monitor_next, orders = pl.pallas_call(
        hand_over_kernel,
        name="hand_over",
        out_shape=tuple(jax.ShapeDtypeStruct(value.shape, f32) for value in held),
        in_specs=[vmem] * 5,
        out_specs=(hbm,) * 5,
        scratch_shapes=[dma((5,))],
    )(*[pltpu.with_memory_space_constraint(value, pltpu.VMEM) for value in held])
    return (
        electric_next,
        magnetic_next,
        slab_next,
        monitor_next.reshape(monitor_spectra.shape),
        orders,
    )


def solution(mesh, order_count=128):
    fields = P(None, None, "gx", "gy")
    spectra = P(None, None, None, "gx", "gy")
    return jax.shard_map(
        functools.partial(per_device, mesh.shape["gx"], mesh.shape["gy"], order_count),
        mesh=mesh,
        in_specs=(fields, fields, P(None, "gx", "gy"), P(), fields, spectra, P()),
        out_specs=(fields, fields, fields, spectra, P("gy", None, None, "gx", None)),
        check_vma=False,
    )
```

```python
import functools
import math

import jax
import jax.numpy as jnp
import numpy as np
from jax import lax
from jax.experimental import pallas as pl
from jax.experimental.pallas import tpu as pltpu
from jax.sharding import PartitionSpec as P

MESH = pl.DeviceIdType.MESH
OX = 64
TIME_STEP = 0.5
OMEGA_LOW = 0.15
OMEGA_HIGH = 0.8
EDGE_MOVES = ((0, -1), (0, 1), (-1, 0), (1, 0), (-1, -1), (1, -1), (-1, 1), (1, 1))


def omegas(freq_count):
    low, high = np.float32(OMEGA_LOW), np.float32(OMEGA_HIGH - OMEGA_LOW)
    return low + high * np.arange(freq_count, dtype=np.float32) / np.float32(freq_count - 1)


def slab_weights(freq_count):
    rows = []
    for step in (1, 2):
        angle = (np.float32(TIME_STEP * step) * omegas(freq_count)).astype(np.float64)
        rows.append(np.concatenate([TIME_STEP * np.cos(angle), -TIME_STEP * np.sin(angle)]))
    return np.stack(rows).astype(np.float32)


def monitor_weights(freq_count):
    rows = []
    for step in (1, 2):
        for lag in (0.0, 0.5):
            angle = (np.float32(TIME_STEP * (step - lag)) * omegas(freq_count)).astype(np.float64)
            rows += [TIME_STEP * np.cos(angle), -TIME_STEP * np.sin(angle)]
    return np.stack(rows).astype(np.float32)


def split_table(table):
    table = table.astype(np.float32)
    lead = table.astype(jnp.bfloat16)
    rest = (table - lead.astype(np.float32)).astype(jnp.bfloat16)
    return np.concatenate([lead, lead], axis=0), rest


def y_tables(gy_count, local_y, order_count):
    length = gy_count * local_y
    orders = np.arange(order_count) - order_count // 2
    inside = 2.0 * np.pi / length * (np.arange(local_y)[:, None] * orders[None, :] % length)
    blocks = 2.0 * np.pi / length * (local_y * np.arange(gy_count)[:, None] * orders[None, :] % length)
    local = np.concatenate([np.cos(inside), np.sin(inside)], axis=1)
    turn = np.stack([np.cos(blocks), np.sin(blocks)], axis=1)
    return split_table(local), turn.astype(np.float32)


def x_local_table(gx_count, local_x, components, full_length):
    length = gx_count * local_x
    orders = np.arange(OX) - OX // 2
    inside = 2.0 * np.pi / length * (np.arange(local_x)[:, None] * orders[None, :] % length)
    scale = 1.0 / math.sqrt(length * full_length)
    cosine, sine = np.cos(inside) * scale, np.sin(inside) * scale
    half, wide = components * local_x, components * OX
    local = np.zeros((128, 2 * wide))
    for c in range(components):
        real = slice(c * local_x, (c + 1) * local_x)
        imag = slice(half + c * local_x, half + (c + 1) * local_x)
        to_real = slice(c * OX, (c + 1) * OX)
        to_imag = slice(wide + c * OX, wide + (c + 1) * OX)
        local[real, to_real], local[real, to_imag] = cosine, -sine
        local[imag, to_real], local[imag, to_imag] = sine, cosine
    return split_table(local)


def x_turn_table(gx_count, local_x, kept):
    length = gx_count * local_x
    orders = np.arange(OX) - OX // 2
    blocks = 2.0 * np.pi / length * (local_x * np.arange(gx_count)[:, None] * orders[None, :] % length)
    turn = np.repeat(np.stack([np.cos(blocks), np.sin(blocks)]), kept, axis=1)
    return np.tile(turn, (1, 1, 2)).astype(np.float32)


def split_dot(value, table, rest):
    lead = value.astype(jnp.bfloat16)
    low = (value - lead.astype(jnp.float32)).astype(jnp.bfloat16)
    return jnp.dot(
        jnp.concatenate([lead, low], axis=1), table, preferred_element_type=jnp.float32
    ) + jnp.dot(lead, rest, preferred_element_type=jnp.float32)


def whole_kernel(
    gx_count,
    gy_count,
    electric,
    magnetic,
    material,
    monitor,
    slab,
    y_lead_in,
    y_rest_in,
    y_turn_in,
    xm_lead_in,
    xm_rest_in,
    xf_lead_in,
    xf_rest_in,
    x_turn_in,
    permittivity,
    wave_index,
    weights,
    slab_table,
    electric_out,
    magnetic_out,
    slab_out,
    monitor_out,
    orders_out,
    field,
    strip,
    classes,
    mbuf,
    rbuf,
    corner,
    edges,
    edges_in,
    edges_x,
    kbuf_m,
    kin_m,
    kbuf_f,
    kin_f,
    kbuf_h,
    kin_h,
    xbuf,
    share,
    share_in,
    records,
    slab_records,
    y_lead,
    y_rest,
    y_turn,
    xm_lead,
    xm_rest,
    xf_lead,
    xf_rest,
    x_turn,
    load_sem,
    strip_send,
    strip_recv,
    edge_send,
    edge_recv,
    a_send,
    a_recv,
    m_send,
    m_recv,
    f_send,
    f_recv,
    h_send,
    h_recv,
    c_send,
    c_recv,
):
    gx = lax.axis_index("gx")
    gy = lax.axis_index("gy")
    kept = kbuf_m.shape[1]
    order_count = gx_count * kept

    def along_gx(step):
        return lax.rem(gx + (step + gx_count), gx_count)

    def along_gy(step):
        return lax.rem(gy + (step + gy_count), gy_count)

    loads = [
        pltpu.make_async_copy(source, target, load_sem.at[i])
        for i, (source, target) in enumerate(
            (
                (material, classes),
                (electric, field.at[0:3, 1:17, 0:8, :]),
                (magnetic, field.at[3:6, 1:17, 0:8, :]),
                (monitor, mbuf),
                (slab, slab_out),
                (y_lead_in, y_lead),
                (y_rest_in, y_rest),
                (y_turn_in, y_turn),
                (xm_lead_in, xm_lead),
                (xm_rest_in, xm_rest),
                (xf_lead_in, xf_lead),
                (xf_rest_in, xf_rest),
                (x_turn_in, x_turn),
            )
        )
    ]
    for load in loads:
        load.start()

    barrier = pltpu.get_barrier_semaphore()

    def greet_x(step, carry):
        pl.semaphore_signal(barrier, inc=1, device_id=(along_gx(step), gy), device_id_type=MESH)
        return carry

    def greet_y(step, carry):
        pl.semaphore_signal(barrier, inc=1, device_id=(gx, along_gy(step)), device_id_type=MESH)
        return carry

    lax.fori_loop(1, gx_count, greet_x, 0)
    lax.fori_loop(1, gy_count, greet_y, 0)
    for dx, dy in EDGE_MOVES[4:]:
        pl.semaphore_signal(
            barrier, inc=1, device_id=(along_gx(dx), along_gy(dy)), device_id_type=MESH
        )

    field[0:6, 0] = jnp.zeros((6, 16, 128), jnp.float32)
    field[0:6, 17] = jnp.zeros((6, 16, 128), jnp.float32)

    loads[0].wait()
    inverses = [1.0 / jnp.full((8, 128), permittivity[i], jnp.float32) for i in range(4)]
    for z in range(16):
        here = classes[z]
        value = jnp.zeros((8, 128), jnp.float32)
        for i in range(4):
            value = value + jnp.where(here == i, inverses[i], 0.0)
        field[6, z + 1, 0:8, :] = value
    loads[1].wait()
    loads[2].wait()

    lane = lax.broadcasted_iota(jnp.int32, (8, 128), 1)
    top = lax.broadcasted_iota(jnp.int32, (8, 128), 0) < 4
    cell = lax.rem(lane, 8)

    def pack(c, carry):
        held = jnp.zeros((8, 128), jnp.float32)
        for z in range(16):
            tile = field[c, z + 1, 0:8, :]
            held = jnp.where(lane // 8 == z, pltpu.roll(tile, (8 * z + 2) % 128, 1), held)
        corner[c] = held
        return carry

    lax.fori_loop(0, 7, pack, 0)

    for t in range(2):
        for side in range(2):
            held = jnp.zeros((8, 128), jnp.float32)
            for i in range(4 - t):
                moved = pltpu.roll(corner[4 * t + i], (2 * i - 2 * side) % 128, 1)
                held = jnp.where(cell // 2 == i, moved, held)
            edges[side, t] = held
    loads[3].wait()

    pl.semaphore_wait(barrier, gx_count - 1 + gy_count - 1 + 4)

    shares = []
    for i, (dx, dy) in enumerate(EDGE_MOVES):
        if dy:
            source, target = edges.at[(1 - dy) // 2], edges_in.at[i]
        else:
            source, target = edges, edges_x.at[(1 + dx) // 2]
        shares.append(
            pltpu.make_async_remote_copy(
                src_ref=source,
                dst_ref=target,
                send_sem=edge_send.at[i],
                recv_sem=edge_recv.at[i],
                device_id=(along_gx(dx), along_gy(dy)),
                device_id_type=MESH,
            )
        )
    strips = []
    for i, (step, first, landing) in enumerate(((-1, 0, 8), (1, 6, 14))):
        strips.append(
            pltpu.make_async_remote_copy(
                src_ref=field.at[:, 1:17, first : first + 2, :],
                dst_ref=field.at[:, 1:17, landing : landing + 2, :],
                send_sem=strip_send.at[i],
                recv_sem=strip_recv.at[i],
                device_id=(along_gx(step), gy),
                device_id_type=MESH,
            )
        )
    for copy in shares[::-1] + strips:
        copy.start()

    def a_copy(w, b, slot):
        return pltpu.make_async_remote_copy(
            src_ref=mbuf.at[w, :, 0:2],
            dst_ref=rbuf.at[b],
            send_sem=a_send.at[slot],
            recv_sem=a_recv.at[b],
            device_id=(gx, w),
            device_id_type=MESH,
        )

    half = gy_count // 2
    far_first = [half]
    for i in range(1, half):
        far_first += [half - i, half + i]
    for step in far_first:
        a_copy(along_gy(step), gy, step).start()
    def own_turn(re, im, b):
        turn = y_turn[b]
        cosine, sine = turn[0:1, :], turn[1:2, :]
        return re * cosine + im * sine, im * cosine - re * sine

    def x_copy(source, target, send_sem, recv_sem, g, own, slot):
        return pltpu.make_async_remote_copy(
            src_ref=source.at[g],
            dst_ref=target.at[own],
            send_sem=send_sem.at[slot],
            recv_sem=recv_sem.at[own],
            device_id=(g, gy),
            device_id_type=MESH,
        )

    def send_x(*kind):
        def body(step, carry):
            x_copy(*kind, along_gx(step), gx, step).start()
            return carry

        lax.fori_loop(1, gx_count, body, 0)
        source, target = kind[:2]
        target[gx] = source[gx]

    def take_x(*kind):
        def body(step, carry):
            x_copy(*kind, along_gx(step), along_gx(-step), step).wait_recv()
            return carry

        lax.fori_loop(1, gx_count, body, 0)

    for load in loads[5:8]:
        load.wait()
    for q in range(gy_count // 4):
        rows = [
            mbuf[w, part, 2:4].reshape(16, 128) for part in range(2) for w in range(4 * q, 4 * q + 4)
        ]
        product = split_dot(jnp.concatenate(rows, axis=0), y_lead[...], y_rest[...])
        a, b = product[0:64], product[64:128]
        re, im = own_turn(
            a[:, 0:order_count] + b[:, order_count:], b[:, 0:order_count] - a[:, order_count:], gy
        )
        turned = jnp.transpose(jnp.concatenate([re, im], axis=0))
        for g in range(gx_count):
            kbuf_h[g, :, 128 * q : 128 * (q + 1)] = turned[kept * g : kept * (g + 1), :]
    send_x(kbuf_h, kin_h, h_send, h_recv)

    for copy in shares:
        copy.wait_recv()

    for c in range(7):
        t, i = c // 4, c % 4

        def shifted(value, to):
            return pltpu.roll(value, (to - 2 * i) % 128, 1)

        behind, ahead = shifted(edges_in[1, t], 0), shifted(edges_in[0, t], 6)
        own = corner[c]
        strip[c, 0:8] = jnp.where(
            cell < 4,
            jnp.where(cell < 2, behind, own),
            jnp.where(cell < 6, pltpu.roll(own, 4, 1), ahead),
        )
        behind = shifted(jnp.where(top, edges_in[6, t], edges_in[7, t]), 0)
        ahead = shifted(jnp.where(top, edges_in[4, t], edges_in[5, t]), 6)
        near_last = shifted(jnp.where(top, edges_x[0, 0, t], edges_x[1, 0, t]), 4)
        near_first = shifted(jnp.where(top, edges_x[0, 1, t], edges_x[1, 1, t]), 2)
        strip[c, 8:16] = jnp.where(
            cell < 4,
            jnp.where(cell < 2, behind, near_first),
            jnp.where(cell < 6, near_last, ahead),
        )
    for copy in strips:
        copy.wait()

    wide_lane = lax.broadcasted_iota(jnp.int32, (16, 128), 1)
    last_lane, first_lane = wide_lane == 127, wide_lane == 0
    last_layer, first_layer = wide_lane >= 120, wide_lane < 8

    def x_ahead(value):
        return pltpu.roll(value, 15, 0)

    def x_behind(value):
        return pltpu.roll(value, 1, 0)

    def strip_h():
        ex, ey, ez = strip[0], strip[1], strip[2]
        ex_up = jnp.where(last_layer, 0.0, pltpu.roll(ex, 120, 1))
        ey_up = jnp.where(last_layer, 0.0, pltpu.roll(ey, 120, 1))
        ez_y, ex_y = pltpu.roll(ez, 127, 1), pltpu.roll(ex, 127, 1)
        strip[3] = strip[3] - TIME_STEP * (ez_y - ez - (ey_up - ey))
        strip[4] = strip[4] - TIME_STEP * ((ex_up - ex) - (x_ahead(ez) - ez))
        strip[5] = strip[5] - TIME_STEP * (x_ahead(ey) - ey - (ex_y - ex))

    def strip_e():
        hx, hy, hz = strip[3], strip[4], strip[5]
        hx_down = jnp.where(first_layer, 0.0, pltpu.roll(hx, 8, 1))
        hy_down = jnp.where(first_layer, 0.0, pltpu.roll(hy, 8, 1))
        hz_y, hx_y = pltpu.roll(hz, 1, 1), pltpu.roll(hx, 1, 1)
        rate = TIME_STEP * strip[6]
        strip[0] = strip[0] + rate * (hz - hz_y - (hy - hy_down))
        strip[1] = strip[1] + rate * ((hx - hx_down) - (hz - x_behind(hz)))
        strip[2] = strip[2] + rate * (hy - x_behind(hy) - (hx - hx_y))

    def main_h(z):
        def y_ahead(value, c):
            edge = pltpu.roll(strip[c], (129 - 8 * z), 1)
            return jnp.where(last_lane, edge, pltpu.roll(value, 127, 1))

        ex, ey, ez = field[0, z], field[1, z], field[2, z]
        ex_up, ey_up = field[0, z + 1], field[1, z + 1]
        field[3, z] = field[3, z] - TIME_STEP * (y_ahead(ez, 2) - ez - (ey_up - ey))
        field[4, z] = field[4, z] - TIME_STEP * ((ex_up - ex) - (x_ahead(ez) - ez))
        field[5, z] = field[5, z] - TIME_STEP * (x_ahead(ey) - ey - (y_ahead(ex, 0) - ex))

    def main_e(z):
        def y_behind(value, c):
            edge = pltpu.roll(strip[c], (135 - 8 * z) % 128, 1)
            return jnp.where(first_lane, edge, pltpu.roll(value, 1, 1))

        hx, hy, hz = field[3, z], field[4, z], field[5, z]
        hx_down, hy_down = field[3, z - 1], field[4, z - 1]
        rate = TIME_STEP * field[6, z]
        field[0, z] = field[0, z] + rate * (hz - y_behind(hz, 5) - (hy - hy_down))
        field[1, z] = field[1, z] + rate * ((hx - hx_down) - (hz - x_behind(hz)))
        field[2, z] = field[2, z] + rate * (hy - x_behind(hy) - (hx - y_behind(hx, 3)))

    def one_step(step, carry):
        for z in range(1, 17):
            main_h(z)
        strip_h()
        for z in range(1, 17):
            main_e(z)
        strip_e()
        for c in range(2):
            slab_records[c, step] = field[c, 9, 0:8, :]
        for c, row in enumerate((0, 1, 3, 4)):
            records[step, c] = field[row, 16, 0:8, :]
        return carry

    lax.fori_loop(0, 2, one_step, 0)

    for load in loads[8:]:
        load.wait()

    product = split_dot(records[...].reshape(64, 128), y_lead[...], y_rest[...])
    re, im = own_turn(product[:, 0:order_count], -product[:, order_count:], gy)
    turned = jnp.transpose(jnp.concatenate([re, im], axis=0))
    for g in range(gx_count):
        kbuf_f[g] = turned[kept * g : kept * (g + 1), :]

    send_x(kbuf_f, kin_f, f_send, f_recv)

    def hand_out(z, carry):
        for c in range(3):
            electric_out[c, z] = field[c, z + 1, 0:8, :]
            magnetic_out[c, z] = field[3 + c, z + 1, 0:8, :]
        return carry

    lax.fori_loop(0, 16, hand_out, 0)
    loads[4].wait()
    slab_held = [[slab_records[c, s] for s in range(2)] for c in range(2)]

    def slab_update(i, carry):
        for j in range(4):
            f = 4 * i + j
            first, second = slab_table[0, f], slab_table[1, f]
            for c in range(2):
                slab_out[c, f] = slab_out[c, f] + (
                    first * slab_held[c][0] + second * slab_held[c][1]
                )
        return carry

    lax.fori_loop(0, slab_out.shape[1] // 4, slab_update, 0)
    held = [[records[s, c] for c in range(4)] for s in range(2)]

    def weights_of(w):
        pick = wave_index[w]
        return [
            [[weights[4 * s + 2 * kind + i, pick] for i in range(2)] for kind in range(2)]
            for s in range(2)
        ]

    def monitor_update(w, carry):
        scale = weights_of(w)
        for i in range(2):
            for c in range(4):
                monitor_out[w, i, c] = mbuf[w, i, c] + (
                    scale[0][c // 2][i] * held[0][c] + scale[1][c // 2][i] * held[1][c]
                )
        return carry

    lax.fori_loop(0, gy_count, monitor_update, 0)

    cosine, sine = x_turn[0], x_turn[1]

    def folded(value):
        total = value[0:8]
        for r in range(8, kept * gx_count, 8):
            total = total + value[r : r + 8]
        return total[0:kept] + total[kept : 2 * kept]

    def x_sums(values, lead, rest, blocks):
        product = split_dot(values, lead[...], rest[...])
        real, imag = [], []
        for j in range(blocks):
            re = product[:, 128 * j : 128 * (j + 1)]
            im = product[:, 128 * (blocks + j) : 128 * (blocks + j + 1)]
            real.append(folded(re * cosine + im * sine))
            imag.append(folded(im * cosine - re * sine))
        return real, imag

    take_x(kbuf_h, kin_h, h_send, h_recv)
    for q in range(gy_count // 4):
        for g in range(gx_count):
            xbuf[q, kept * g : kept * (g + 1), :] = kin_h[g, :, 128 * q : 128 * (q + 1)]
    for q in range(gy_count // 4):
        h_real, h_imag = x_sums(xbuf[q], xf_lead, xf_rest, 4)
        for j in range(4):
            share[4 * q + j, :, 128:256] = h_real[j]
            share[4 * q + j, :, 384:512] = h_imag[j]

    take_x(kbuf_f, kin_f, f_send, f_recv)
    for g in range(gx_count):
        xbuf[0, kept * g : kept * (g + 1), :] = kin_f[g]
    f_real, f_imag = x_sums(xbuf[0], xf_lead, xf_rest, 4)

    def weigh(w, carry):
        scale = weights_of(w)
        for kind in range(2):
            (r0, i0), (r1, i1) = scale[0][kind], scale[1][kind]
            re0, im0, re1, im1 = f_real[kind], f_imag[kind], f_real[2 + kind], f_imag[2 + kind]
            real = (r0 * re0 - i0 * im0) + (r1 * re1 - i1 * im1)
            imag = (r0 * im0 + i0 * re0) + (r1 * im1 + i1 * re1)
            first, second = 128 * kind, 256 + 128 * kind
            if kind:
                real, imag = real + share[w, :, 128:256], imag + share[w, :, 384:512]
            share[w, :, first : first + 128] = real
            share[w, :, second : second + 128] = imag
        return carry

    lax.fori_loop(0, gy_count, weigh, 0)

    def c_copy(w, b, slot):
        return pltpu.make_async_remote_copy(
            src_ref=share.at[w],
            dst_ref=share_in.at[b],
            send_sem=c_send.at[slot],
            recv_sem=c_recv.at[b],
            device_id=(gx, w),
            device_id_type=MESH,
        )

    for step in far_first:
        c_copy(along_gy(step), gy, step).start()

    def y_part(blocks, owners, real, imag):
        rows = jnp.concatenate([block.reshape(32, 128) for block in blocks], axis=0)
        product = split_dot(rows, y_lead[...], y_rest[...])
        for i, b in enumerate(owners):
            a, c = product[32 * i : 32 * i + 16], product[32 * i + 16 : 32 * i + 32]
            re = a[:, 0:order_count] + c[:, order_count:]
            im = c[:, 0:order_count] - a[:, order_count:]
            re, im = own_turn(re, im, b)
            real, imag = real + re, imag + im
        return real, imag

    real = jnp.zeros((16, order_count), jnp.float32)
    imag = real
    arriving = [0] + far_first[::-1]
    for i in range(0, gy_count, 4):
        blocks, owners = [], []
        for step in arriving[i : i + 4]:
            b = along_gy(-step)
            if step:
                a_copy(along_gy(step), b, step).wait_recv()
                blocks.append(rbuf[b])
            else:
                blocks.append(mbuf[b, :, 0:2])
            owners.append(b)
        real, imag = y_part(blocks, owners, real, imag)

    spectrum = jnp.concatenate([real, imag, jnp.zeros((96, order_count), jnp.float32)], axis=0)
    turned = jnp.transpose(spectrum)
    for g in range(gx_count):
        kbuf_m[g] = turned[kept * g : kept * (g + 1), :]
    send_x(kbuf_m, kin_m, m_send, m_recv)

    total = share[gy]
    for step in far_first[::-1]:
        b = along_gy(-step)
        c_copy(along_gy(step), b, step).wait_recv()
        total = total + share_in[b]

    take_x(kbuf_m, kin_m, m_send, m_recv)
    for g in range(gx_count):
        xbuf[1, kept * g : kept * (g + 1), :] = kin_m[g]
    m_real, m_imag = x_sums(xbuf[1], xm_lead, xm_rest, 1)
    for part, block in enumerate((m_real[0], m_imag[0])):
        for kind in range(2):
            first = 128 * (2 * part + kind)
            value = total[:, first : first + 128]
            if not kind:
                value = value + block
            for c in range(2):
                orders_out[0, part, 2 * kind + c] = value[:, c * OX : (c + 1) * OX]

    for copy in shares:
        copy.wait_send()

    def sent_y(step, carry):
        a_copy(along_gy(step), gy, step).wait_send()
        c_copy(along_gy(step), gy, step).wait_send()
        return carry

    def sent_x(step, carry):
        x_copy(kbuf_f, kin_f, f_send, f_recv, along_gx(step), gx, step).wait_send()
        x_copy(kbuf_m, kin_m, m_send, m_recv, along_gx(step), gx, step).wait_send()
        x_copy(kbuf_h, kin_h, h_send, h_recv, along_gx(step), gx, step).wait_send()
        return carry

    lax.fori_loop(1, gy_count, sent_y, 0)
    lax.fori_loop(1, gx_count, sent_x, 0)


def hand_over_kernel(*refs):
    count = len(refs) // 2
    copies = [
        pltpu.make_async_copy(source, target, refs[-1].at[i])
        for i, (source, target) in enumerate(zip(refs[:count], refs[count:-1]))
    ]
    for copy in copies:
        copy.start()
    for copy in copies:
        copy.wait()


def per_device(
    gx_count,
    gy_count,
    order_count,
    electric,
    magnetic,
    material,
    permittivity,
    slab_spectra,
    monitor_spectra,
    wave_index,
):
    freq_count = slab_spectra.shape[1] // 2
    kept = order_count // gx_count
    (y_lead, y_rest), y_turn = y_tables(gy_count, 128, order_count)
    xm_lead, xm_rest = x_local_table(gx_count, 8, 2, gy_count * 128)
    xf_lead, xf_rest = x_local_table(gx_count, 8, 8, gy_count * 128)
    x_turn = x_turn_table(gx_count, 8, kept)
    tables = [y_lead, y_rest, y_turn, xm_lead, xm_rest, xf_lead, xf_rest, x_turn]
    hbm = pl.BlockSpec(memory_space=pl.ANY)
    vmem = pl.BlockSpec(memory_space=pltpu.VMEM)
    smem = pl.BlockSpec(memory_space=pltpu.SMEM)
    f32 = jnp.float32
    dma = pltpu.SemaphoreType.DMA
    held = pl.pallas_call(
        functools.partial(whole_kernel, gx_count, gy_count),
        name="leapfrog_orders",
        out_shape=(
            pltpu.VMEM(electric.shape, f32),
            pltpu.VMEM(magnetic.shape, f32),
            pltpu.VMEM(slab_spectra.shape, f32),
            pltpu.VMEM(monitor_spectra.shape, f32),
            pltpu.VMEM((1, 2, 4, kept, OX), f32),
        ),
        in_specs=[hbm] * 13 + [smem] * 4,
        out_specs=(vmem,) * 5,
        scratch_shapes=[
            pltpu.VMEM((7, 18, 16, 128), f32),
            pltpu.VMEM((7, 16, 128), f32),
            pltpu.VMEM((16, 8, 128), jnp.int32),
            pltpu.VMEM((gy_count, 2, 4, 8, 128), f32),
            pltpu.VMEM((gy_count, 2, 2, 8, 128), f32),
            pltpu.VMEM((7, 8, 128), f32),
            pltpu.VMEM((2, 2, 8, 128), f32),
            pltpu.VMEM((8, 2, 8, 128), f32),
            pltpu.VMEM((2, 2, 2, 8, 128), f32),
            pltpu.VMEM((gx_count, kept, 128), f32),
            pltpu.VMEM((gx_count, kept, 128), f32),
            pltpu.VMEM((gx_count, kept, 128), f32),
            pltpu.VMEM((gx_count, kept, 128), f32),
            pltpu.VMEM((gx_count, kept, 32 * gy_count), f32),
            pltpu.VMEM((gx_count, kept, 32 * gy_count), f32),
            pltpu.VMEM((4, gx_count * kept, 128), f32),
            pltpu.VMEM((gy_count, kept, 512), f32),
            pltpu.VMEM((gy_count, kept, 512), f32),
            pltpu.VMEM((2, 4, 8, 128), f32),
            pltpu.VMEM((2, 2, 8, 128), f32),
        ]
        + [pltpu.VMEM(table.shape, table.dtype) for table in tables]
        + [
            dma((13,)),
            dma((2,)),
            dma((2,)),
            dma((8,)),
            dma((8,)),
            dma((gy_count,)),
            dma((gy_count,)),
            dma((gx_count,)),
            dma((gx_count,)),
            dma((gx_count,)),
            dma((gx_count,)),
            dma((gx_count,)),
            dma((gx_count,)),
            dma((gy_count,)),
            dma((gy_count,)),
        ],
        compiler_params=pltpu.CompilerParams(collective_id=0, has_side_effects=True),
    )(
        electric,
        magnetic,
        material,
        monitor_spectra,
        slab_spectra,
        *[jnp.asarray(table) for table in tables],
        permittivity,
        wave_index,
        jnp.asarray(monitor_weights(freq_count)),
        jnp.asarray(slab_weights(freq_count)),
    )
    electric_next, magnetic_next, slab_next, monitor_next, orders = pl.pallas_call(
        hand_over_kernel,
        name="hand_over",
        out_shape=tuple(jax.ShapeDtypeStruct(value.shape, f32) for value in held),
        in_specs=[vmem] * 5,
        out_specs=(hbm,) * 5,
        scratch_shapes=[dma((5,))],
    )(*[pltpu.with_memory_space_constraint(value, pltpu.VMEM) for value in held])
    return (
        electric_next,
        magnetic_next,
        slab_next,
        monitor_next,
        orders,
    )


def solution(mesh, order_count=128):
    fields = P(None, None, "gx", "gy")
    spectra = P(None, None, None, "gx", "gy")
    return jax.shard_map(
        functools.partial(per_device, mesh.shape["gx"], mesh.shape["gy"], order_count),
        mesh=mesh,
        in_specs=(fields, fields, P(None, "gx", "gy"), P(), fields, spectra, P()),
        out_specs=(fields, fields, fields, spectra, P("gy", None, None, "gx", None)),
        check_vma=False,
    )
```

```python
import functools
import math

import jax
import jax.numpy as jnp
import numpy as np
from jax import lax
from jax.experimental import pallas as pl
from jax.experimental.pallas import tpu as pltpu
from jax.sharding import PartitionSpec as P

MESH = pl.DeviceIdType.MESH
OX = 64
TIME_STEP = 0.5
OMEGA_LOW = 0.15
OMEGA_HIGH = 0.8
EDGE_MOVES = ((0, -1), (0, 1), (-1, 0), (1, 0), (-1, -1), (1, -1), (-1, 1), (1, 1))


def omegas(freq_count):
    low, high = np.float32(OMEGA_LOW), np.float32(OMEGA_HIGH - OMEGA_LOW)
    return low + high * np.arange(freq_count, dtype=np.float32) / np.float32(freq_count - 1)


def slab_weights(freq_count):
    rows = []
    for step in (1, 2):
        angle = (np.float32(TIME_STEP * step) * omegas(freq_count)).astype(np.float64)
        rows.append(np.concatenate([TIME_STEP * np.cos(angle), -TIME_STEP * np.sin(angle)]))
    return np.stack(rows).astype(np.float32)


def monitor_weights(freq_count):
    rows = []
    for step in (1, 2):
        for lag in (0.0, 0.5):
            angle = (np.float32(TIME_STEP * (step - lag)) * omegas(freq_count)).astype(np.float64)
            rows += [TIME_STEP * np.cos(angle), -TIME_STEP * np.sin(angle)]
    return np.stack(rows).astype(np.float32)


def split_table(table):
    table = table.astype(np.float32)
    lead = table.astype(jnp.bfloat16)
    rest = (table - lead.astype(np.float32)).astype(jnp.bfloat16)
    return np.concatenate([lead, lead], axis=0), rest


def y_tables(gy_count, local_y, order_count):
    length = gy_count * local_y
    orders = np.arange(order_count) - order_count // 2
    inside = 2.0 * np.pi / length * (np.arange(local_y)[:, None] * orders[None, :] % length)
    blocks = 2.0 * np.pi / length * (local_y * np.arange(gy_count)[:, None] * orders[None, :] % length)
    local = np.concatenate([np.cos(inside), np.sin(inside)], axis=1)
    turn = np.stack([np.cos(blocks), np.sin(blocks)], axis=1)
    return split_table(local), turn.astype(np.float32)


def x_local_table(gx_count, local_x, components, full_length):
    length = gx_count * local_x
    orders = np.arange(OX) - OX // 2
    inside = 2.0 * np.pi / length * (np.arange(local_x)[:, None] * orders[None, :] % length)
    scale = 1.0 / math.sqrt(length * full_length)
    cosine, sine = np.cos(inside) * scale, np.sin(inside) * scale
    half, wide = components * local_x, components * OX
    local = np.zeros((128, 2 * wide))
    for c in range(components):
        real = slice(c * local_x, (c + 1) * local_x)
        imag = slice(half + c * local_x, half + (c + 1) * local_x)
        to_real = slice(c * OX, (c + 1) * OX)
        to_imag = slice(wide + c * OX, wide + (c + 1) * OX)
        local[real, to_real], local[real, to_imag] = cosine, -sine
        local[imag, to_real], local[imag, to_imag] = sine, cosine
    return split_table(local)


def x_turn_table(gx_count, local_x, kept):
    length = gx_count * local_x
    orders = np.arange(OX) - OX // 2
    blocks = 2.0 * np.pi / length * (local_x * np.arange(gx_count)[:, None] * orders[None, :] % length)
    turn = np.repeat(np.stack([np.cos(blocks), np.sin(blocks)]), kept, axis=1)
    return np.tile(turn, (1, 1, 2)).astype(np.float32)


def split_dot(value, table, rest):
    lead = value.astype(jnp.bfloat16)
    low = (value - lead.astype(jnp.float32)).astype(jnp.bfloat16)
    return jnp.dot(
        jnp.concatenate([lead, low], axis=1), table, preferred_element_type=jnp.float32
    ) + jnp.dot(lead, rest, preferred_element_type=jnp.float32)


def whole_kernel(
    gx_count,
    gy_count,
    electric,
    magnetic,
    material,
    monitor,
    slab,
    y_lead_in,
    y_rest_in,
    y_turn_in,
    xm_lead_in,
    xm_rest_in,
    xf_lead_in,
    xf_rest_in,
    x_turn_in,
    permittivity,
    wave_index,
    weights,
    slab_table,
    electric_out,
    magnetic_out,
    slab_out,
    monitor_out,
    orders_out,
    field,
    strip,
    classes,
    mbuf,
    rbuf,
    corner,
    edges,
    edges_in,
    edges_x,
    kbuf_m,
    kin_m,
    kbuf_f,
    kin_f,
    kbuf_h,
    kin_h,
    xbuf,
    share,
    share_in,
    records,
    slab_records,
    y_lead,
    y_rest,
    y_turn,
    xm_lead,
    xm_rest,
    xf_lead,
    xf_rest,
    x_turn,
    load_sem,
    strip_send,
    strip_recv,
    edge_send,
    edge_recv,
    a_send,
    a_recv,
    m_send,
    m_recv,
    f_send,
    f_recv,
    h_send,
    h_recv,
    c_send,
    c_recv,
):
    gx = lax.axis_index("gx")
    gy = lax.axis_index("gy")
    kept = kbuf_m.shape[1]
    order_count = gx_count * kept

    def along_gx(step):
        return lax.rem(gx + (step + gx_count), gx_count)

    def along_gy(step):
        return lax.rem(gy + (step + gy_count), gy_count)

    loads = [
        pltpu.make_async_copy(source, target, load_sem.at[i])
        for i, (source, target) in enumerate(
            (
                (material, classes),
                (electric, field.at[0:3, 1:17, 0:8, :]),
                (magnetic, field.at[3:6, 1:17, 0:8, :]),
                (monitor, mbuf),
                (slab, slab_out),
                (y_lead_in, y_lead),
                (y_rest_in, y_rest),
                (y_turn_in, y_turn),
                (xm_lead_in, xm_lead),
                (xm_rest_in, xm_rest),
                (xf_lead_in, xf_lead),
                (xf_rest_in, xf_rest),
                (x_turn_in, x_turn),
            )
        )
    ]
    for load in loads:
        load.start()

    barrier = pltpu.get_barrier_semaphore()

    def greet_x(step, carry):
        pl.semaphore_signal(barrier, inc=1, device_id=(along_gx(step), gy), device_id_type=MESH)
        return carry

    def greet_y(step, carry):
        pl.semaphore_signal(barrier, inc=1, device_id=(gx, along_gy(step)), device_id_type=MESH)
        return carry

    lax.fori_loop(1, gx_count, greet_x, 0)
    lax.fori_loop(1, gy_count, greet_y, 0)
    for dx, dy in EDGE_MOVES[4:]:
        pl.semaphore_signal(
            barrier, inc=1, device_id=(along_gx(dx), along_gy(dy)), device_id_type=MESH
        )

    field[0:6, 0] = jnp.zeros((6, 16, 128), jnp.float32)
    field[0:6, 17] = jnp.zeros((6, 16, 128), jnp.float32)

    loads[0].wait()
    inverses = [1.0 / jnp.full((8, 128), permittivity[i], jnp.float32) for i in range(4)]
    for z in range(16):
        here = classes[z]
        value = jnp.zeros((8, 128), jnp.float32)
        for i in range(4):
            value = value + jnp.where(here == i, inverses[i], 0.0)
        field[6, z + 1, 0:8, :] = value
    loads[1].wait()
    loads[2].wait()

    lane = lax.broadcasted_iota(jnp.int32, (8, 128), 1)
    top = lax.broadcasted_iota(jnp.int32, (8, 128), 0) < 4
    cell = lax.rem(lane, 8)

    def pack(c, carry):
        held = jnp.zeros((8, 128), jnp.float32)
        for z in range(16):
            tile = field[c, z + 1, 0:8, :]
            held = jnp.where(lane // 8 == z, pltpu.roll(tile, (8 * z + 2) % 128, 1), held)
        corner[c] = held
        return carry

    lax.fori_loop(0, 7, pack, 0)

    for t in range(2):
        for side in range(2):
            held = jnp.zeros((8, 128), jnp.float32)
            for i in range(4 - t):
                moved = pltpu.roll(corner[4 * t + i], (2 * i - 2 * side) % 128, 1)
                held = jnp.where(cell // 2 == i, moved, held)
            edges[side, t] = held
    loads[3].wait()

    pl.semaphore_wait(barrier, gx_count - 1 + gy_count - 1 + 4)

    shares = []
    for i, (dx, dy) in enumerate(EDGE_MOVES):
        if dy:
            source, target = edges.at[(1 - dy) // 2], edges_in.at[i]
        else:
            source, target = edges, edges_x.at[(1 + dx) // 2]
        shares.append(
            pltpu.make_async_remote_copy(
                src_ref=source,
                dst_ref=target,
                send_sem=edge_send.at[i],
                recv_sem=edge_recv.at[i],
                device_id=(along_gx(dx), along_gy(dy)),
                device_id_type=MESH,
            )
        )
    strips = []
    for i, (step, first, landing) in enumerate(((-1, 0, 8), (1, 6, 14))):
        strips.append(
            pltpu.make_async_remote_copy(
                src_ref=field.at[:, 1:17, first : first + 2, :],
                dst_ref=field.at[:, 1:17, landing : landing + 2, :],
                send_sem=strip_send.at[i],
                recv_sem=strip_recv.at[i],
                device_id=(along_gx(step), gy),
                device_id_type=MESH,
            )
        )
    for copy in shares[::-1] + strips:
        copy.start()

    def a_copy(w, b, slot):
        return pltpu.make_async_remote_copy(
            src_ref=mbuf.at[w, :, 0:3],
            dst_ref=rbuf.at[b],
            send_sem=a_send.at[slot],
            recv_sem=a_recv.at[b],
            device_id=(gx, w),
            device_id_type=MESH,
        )

    half = gy_count // 2
    far_first = [half]
    for i in range(1, half):
        far_first += [half - i, half + i]
    for step in far_first:
        a_copy(along_gy(step), gy, step).start()
    def own_turn(re, im, b):
        turn = y_turn[b]
        cosine, sine = turn[0:1, :], turn[1:2, :]
        return re * cosine + im * sine, im * cosine - re * sine

    def x_copy(source, target, send_sem, recv_sem, g, own, slot):
        return pltpu.make_async_remote_copy(
            src_ref=source.at[g],
            dst_ref=target.at[own],
            send_sem=send_sem.at[slot],
            recv_sem=recv_sem.at[own],
            device_id=(g, gy),
            device_id_type=MESH,
        )

    def send_x(*kind):
        def body(step, carry):
            x_copy(*kind, along_gx(step), gx, step).start()
            return carry

        lax.fori_loop(1, gx_count, body, 0)
        source, target = kind[:2]
        target[gx] = source[gx]

    def take_x(*kind):
        def body(step, carry):
            x_copy(*kind, along_gx(step), along_gx(-step), step).wait_recv()
            return carry

        lax.fori_loop(1, gx_count, body, 0)

    for load in loads[5:8]:
        load.wait()
    for q in range(gy_count // 8):
        rows = [mbuf[w, part, 3] for part in range(2) for w in range(8 * q, 8 * q + 8)]
        product = split_dot(jnp.concatenate(rows, axis=0), y_lead[...], y_rest[...])
        a, b = product[0:64], product[64:128]
        re, im = own_turn(
            a[:, 0:order_count] + b[:, order_count:], b[:, 0:order_count] - a[:, order_count:], gy
        )
        turned = jnp.transpose(jnp.concatenate([re, im], axis=0))
        for g in range(gx_count):
            kbuf_h[g, :, 128 * q : 128 * (q + 1)] = turned[kept * g : kept * (g + 1), :]
    send_x(kbuf_h, kin_h, h_send, h_recv)

    for copy in shares:
        copy.wait_recv()

    for c in range(7):
        t, i = c // 4, c % 4

        def shifted(value, to):
            return pltpu.roll(value, (to - 2 * i) % 128, 1)

        behind, ahead = shifted(edges_in[1, t], 0), shifted(edges_in[0, t], 6)
        own = corner[c]
        strip[c, 0:8] = jnp.where(
            cell < 4,
            jnp.where(cell < 2, behind, own),
            jnp.where(cell < 6, pltpu.roll(own, 4, 1), ahead),
        )
        behind = shifted(jnp.where(top, edges_in[6, t], edges_in[7, t]), 0)
        ahead = shifted(jnp.where(top, edges_in[4, t], edges_in[5, t]), 6)
        near_last = shifted(jnp.where(top, edges_x[0, 0, t], edges_x[1, 0, t]), 4)
        near_first = shifted(jnp.where(top, edges_x[0, 1, t], edges_x[1, 1, t]), 2)
        strip[c, 8:16] = jnp.where(
            cell < 4,
            jnp.where(cell < 2, behind, near_first),
            jnp.where(cell < 6, near_last, ahead),
        )
    for copy in strips:
        copy.wait()

    wide_lane = lax.broadcasted_iota(jnp.int32, (16, 128), 1)
    last_lane, first_lane = wide_lane == 127, wide_lane == 0
    last_layer, first_layer = wide_lane >= 120, wide_lane < 8

    def x_ahead(value):
        return pltpu.roll(value, 15, 0)

    def x_behind(value):
        return pltpu.roll(value, 1, 0)

    def strip_h():
        ex, ey, ez = strip[0], strip[1], strip[2]
        ex_up = jnp.where(last_layer, 0.0, pltpu.roll(ex, 120, 1))
        ey_up = jnp.where(last_layer, 0.0, pltpu.roll(ey, 120, 1))
        ez_y, ex_y = pltpu.roll(ez, 127, 1), pltpu.roll(ex, 127, 1)
        strip[3] = strip[3] - TIME_STEP * (ez_y - ez - (ey_up - ey))
        strip[4] = strip[4] - TIME_STEP * ((ex_up - ex) - (x_ahead(ez) - ez))
        strip[5] = strip[5] - TIME_STEP * (x_ahead(ey) - ey - (ex_y - ex))

    def strip_e():
        hx, hy, hz = strip[3], strip[4], strip[5]
        hx_down = jnp.where(first_layer, 0.0, pltpu.roll(hx, 8, 1))
        hy_down = jnp.where(first_layer, 0.0, pltpu.roll(hy, 8, 1))
        hz_y, hx_y = pltpu.roll(hz, 1, 1), pltpu.roll(hx, 1, 1)
        rate = TIME_STEP * strip[6]
        strip[0] = strip[0] + rate * (hz - hz_y - (hy - hy_down))
        strip[1] = strip[1] + rate * ((hx - hx_down) - (hz - x_behind(hz)))
        strip[2] = strip[2] + rate * (hy - x_behind(hy) - (hx - hx_y))

    def main_h(z):
        def y_ahead(value, c):
            edge = pltpu.roll(strip[c], (129 - 8 * z), 1)
            return jnp.where(last_lane, edge, pltpu.roll(value, 127, 1))

        ex, ey, ez = field[0, z], field[1, z], field[2, z]
        ex_up, ey_up = field[0, z + 1], field[1, z + 1]
        field[3, z] = field[3, z] - TIME_STEP * (y_ahead(ez, 2) - ez - (ey_up - ey))
        field[4, z] = field[4, z] - TIME_STEP * ((ex_up - ex) - (x_ahead(ez) - ez))
        field[5, z] = field[5, z] - TIME_STEP * (x_ahead(ey) - ey - (y_ahead(ex, 0) - ex))

    def main_e(z):
        def y_behind(value, c):
            edge = pltpu.roll(strip[c], (135 - 8 * z) % 128, 1)
            return jnp.where(first_lane, edge, pltpu.roll(value, 1, 1))

        hx, hy, hz = field[3, z], field[4, z], field[5, z]
        hx_down, hy_down = field[3, z - 1], field[4, z - 1]
        rate = TIME_STEP * field[6, z]
        field[0, z] = field[0, z] + rate * (hz - y_behind(hz, 5) - (hy - hy_down))
        field[1, z] = field[1, z] + rate * ((hx - hx_down) - (hz - x_behind(hz)))
        field[2, z] = field[2, z] + rate * (hy - x_behind(hy) - (hx - y_behind(hx, 3)))

    def one_step(step, carry):
        for z in range(1, 17):
            main_h(z)
        strip_h()
        for z in range(1, 17):
            main_e(z)
        strip_e()
        for c in range(2):
            slab_records[c, step] = field[c, 9, 0:8, :]
        for c, row in enumerate((0, 1, 3, 4)):
            records[step, c] = field[row, 16, 0:8, :]
        return carry

    lax.fori_loop(0, 2, one_step, 0)

    for load in loads[8:]:
        load.wait()

    product = split_dot(records[...].reshape(64, 128), y_lead[...], y_rest[...])
    re, im = own_turn(product[:, 0:order_count], -product[:, order_count:], gy)
    turned = jnp.transpose(jnp.concatenate([re, im], axis=0))
    for g in range(gx_count):
        kbuf_f[g] = turned[kept * g : kept * (g + 1), :]

    send_x(kbuf_f, kin_f, f_send, f_recv)

    def hand_out(z, carry):
        for c in range(3):
            electric_out[c, z] = field[c, z + 1, 0:8, :]
            magnetic_out[c, z] = field[3 + c, z + 1, 0:8, :]
        return carry

    lax.fori_loop(0, 16, hand_out, 0)
    loads[4].wait()
    slab_held = [[slab_records[c, s] for s in range(2)] for c in range(2)]

    def slab_update(i, carry):
        for j in range(4):
            f = 4 * i + j
            first, second = slab_table[0, f], slab_table[1, f]
            for c in range(2):
                slab_out[c, f] = slab_out[c, f] + (
                    first * slab_held[c][0] + second * slab_held[c][1]
                )
        return carry

    lax.fori_loop(0, slab_out.shape[1] // 4, slab_update, 0)
    held = [[records[s, c] for c in range(4)] for s in range(2)]

    def weights_of(w):
        pick = wave_index[w]
        return [
            [[weights[4 * s + 2 * kind + i, pick] for i in range(2)] for kind in range(2)]
            for s in range(2)
        ]

    def monitor_update(w, carry):
        scale = weights_of(w)
        for i in range(2):
            for c in range(4):
                monitor_out[w, i, c] = mbuf[w, i, c] + (
                    scale[0][c // 2][i] * held[0][c] + scale[1][c // 2][i] * held[1][c]
                )
        return carry


    cosine, sine = x_turn[0], x_turn[1]

    def folded(value):
        total = value[0:8]
        for r in range(8, kept * gx_count, 8):
            total = total + value[r : r + 8]
        return total[0:kept] + total[kept : 2 * kept]

    def x_sums(values, lead, rest, blocks):
        product = split_dot(values, lead[...], rest[...])
        real, imag = [], []
        for j in range(blocks):
            re = product[:, 128 * j : 128 * (j + 1)]
            im = product[:, 128 * (blocks + j) : 128 * (blocks + j + 1)]
            real.append(folded(re * cosine + im * sine))
            imag.append(folded(im * cosine - re * sine))
        return real, imag

    def y_part(blocks, owners, real, imag):
        rows = jnp.concatenate([block.reshape(48, 128) for block in blocks], axis=0)
        product = split_dot(rows, y_lead[...], y_rest[...])
        for i, b in enumerate(owners):
            a, c = product[48 * i : 48 * i + 24], product[48 * i + 24 : 48 * i + 48]
            re = a[:, 0:order_count] + c[:, order_count:]
            im = c[:, 0:order_count] - a[:, order_count:]
            re, im = own_turn(re, im, b)
            real, imag = real + re, imag + im
        return real, imag

    real = jnp.zeros((24, order_count), jnp.float32)
    imag = real
    arriving = [0] + far_first[::-1]
    for i in range(0, gy_count, 4):
        blocks, owners = [], []
        for step in arriving[i : i + 4]:
            b = along_gy(-step)
            if step:
                a_copy(along_gy(step), b, step).wait_recv()
                blocks.append(rbuf[b])
            else:
                blocks.append(mbuf[b, :, 0:3])
            owners.append(b)
        real, imag = y_part(blocks, owners, real, imag)

    spare = jnp.zeros((72, order_count), jnp.float32)
    spectrum = jnp.concatenate([real, spare[0:8], imag, spare], axis=0)
    turned = jnp.transpose(spectrum)
    for g in range(gx_count):
        kbuf_m[g] = turned[kept * g : kept * (g + 1), :]
    send_x(kbuf_m, kin_m, m_send, m_recv)

    upper = lax.broadcasted_iota(jnp.int32, (kept, 128), 1) >= OX
    take_x(kbuf_h, kin_h, h_send, h_recv)
    for q in range(gy_count // 8):
        for g in range(gx_count):
            xbuf[q, kept * g : kept * (g + 1), :] = kin_h[g, :, 128 * q : 128 * (q + 1)]
    for q in range(gy_count // 8):
        h_real, h_imag = x_sums(xbuf[q], xf_lead, xf_rest, 4)
        for j in range(8):
            for first, blocks in ((128, h_real), (384, h_imag)):
                block = blocks[j // 2]
                block = block if j % 2 else pltpu.roll(block, OX, 1)
                share[8 * q + j, :, first : first + 128] = jnp.where(upper, block, 0.0)

    take_x(kbuf_f, kin_f, f_send, f_recv)
    for g in range(gx_count):
        xbuf[0, kept * g : kept * (g + 1), :] = kin_f[g]
    f_real, f_imag = x_sums(xbuf[0], xf_lead, xf_rest, 4)

    def weigh(w, carry):
        scale = weights_of(w)
        for kind in range(2):
            (r0, i0), (r1, i1) = scale[0][kind], scale[1][kind]
            re0, im0, re1, im1 = f_real[kind], f_imag[kind], f_real[2 + kind], f_imag[2 + kind]
            real = (r0 * re0 - i0 * im0) + (r1 * re1 - i1 * im1)
            imag = (r0 * im0 + i0 * re0) + (r1 * im1 + i1 * re1)
            first, second = 128 * kind, 256 + 128 * kind
            if kind:
                real, imag = real + share[w, :, 128:256], imag + share[w, :, 384:512]
            share[w, :, first : first + 128] = real
            share[w, :, second : second + 128] = imag
        return carry

    lax.fori_loop(0, gy_count, weigh, 0)

    def c_copy(w, b, slot):
        return pltpu.make_async_remote_copy(
            src_ref=share.at[w],
            dst_ref=share_in.at[b],
            send_sem=c_send.at[slot],
            recv_sem=c_recv.at[b],
            device_id=(gx, w),
            device_id_type=MESH,
        )

    for step in far_first:
        c_copy(along_gy(step), gy, step).start()
    lax.fori_loop(0, gy_count, monitor_update, 0)

    take_x(kbuf_m, kin_m, m_send, m_recv)
    for g in range(gx_count):
        xbuf[1, kept * g : kept * (g + 1), :] = kin_m[g]
    m_real, m_imag = x_sums(xbuf[1], xm_lead, xm_rest, 2)
    total = share[gy]
    for step in far_first[::-1]:
        b = along_gy(-step)
        c_copy(along_gy(step), b, step).wait_recv()
        total = total + share_in[b]

    for part, blocks in enumerate((m_real, m_imag)):
        for kind in range(2):
            first = 128 * (2 * part + kind)
            value = total[:, first : first + 128] + blocks[kind]
            for c in range(2):
                orders_out[0, part, 2 * kind + c] = value[:, c * OX : (c + 1) * OX]

    for copy in shares:
        copy.wait_send()

    def sent_y(step, carry):
        a_copy(along_gy(step), gy, step).wait_send()
        c_copy(along_gy(step), gy, step).wait_send()
        return carry

    def sent_x(step, carry):
        x_copy(kbuf_f, kin_f, f_send, f_recv, along_gx(step), gx, step).wait_send()
        x_copy(kbuf_m, kin_m, m_send, m_recv, along_gx(step), gx, step).wait_send()
        x_copy(kbuf_h, kin_h, h_send, h_recv, along_gx(step), gx, step).wait_send()
        return carry

    lax.fori_loop(1, gy_count, sent_y, 0)
    lax.fori_loop(1, gx_count, sent_x, 0)


def hand_over_kernel(*refs):
    count = len(refs) // 2
    copies = [
        pltpu.make_async_copy(source, target, refs[-1].at[i])
        for i, (source, target) in enumerate(zip(refs[:count], refs[count:-1]))
    ]
    for copy in copies:
        copy.start()
    for copy in copies:
        copy.wait()


def per_device(
    gx_count,
    gy_count,
    order_count,
    electric,
    magnetic,
    material,
    permittivity,
    slab_spectra,
    monitor_spectra,
    wave_index,
):
    freq_count = slab_spectra.shape[1] // 2
    kept = order_count // gx_count
    (y_lead, y_rest), y_turn = y_tables(gy_count, 128, order_count)
    xm_lead, xm_rest = x_local_table(gx_count, 8, 4, gy_count * 128)
    xf_lead, xf_rest = x_local_table(gx_count, 8, 8, gy_count * 128)
    x_turn = x_turn_table(gx_count, 8, kept)
    tables = [y_lead, y_rest, y_turn, xm_lead, xm_rest, xf_lead, xf_rest, x_turn]
    hbm = pl.BlockSpec(memory_space=pl.ANY)
    vmem = pl.BlockSpec(memory_space=pltpu.VMEM)
    smem = pl.BlockSpec(memory_space=pltpu.SMEM)
    f32 = jnp.float32
    dma = pltpu.SemaphoreType.DMA
    held = pl.pallas_call(
        functools.partial(whole_kernel, gx_count, gy_count),
        name="leapfrog_orders",
        out_shape=(
            pltpu.VMEM(electric.shape, f32),
            pltpu.VMEM(magnetic.shape, f32),
            pltpu.VMEM(slab_spectra.shape, f32),
            pltpu.VMEM(monitor_spectra.shape, f32),
            pltpu.VMEM((1, 2, 4, kept, OX), f32),
        ),
        in_specs=[hbm] * 13 + [smem] * 4,
        out_specs=(vmem,) * 5,
        scratch_shapes=[
            pltpu.VMEM((7, 18, 16, 128), f32),
            pltpu.VMEM((7, 16, 128), f32),
            pltpu.VMEM((16, 8, 128), jnp.int32),
            pltpu.VMEM((gy_count, 2, 4, 8, 128), f32),
            pltpu.VMEM((gy_count, 2, 3, 8, 128), f32),
            pltpu.VMEM((7, 8, 128), f32),
            pltpu.VMEM((2, 2, 8, 128), f32),
            pltpu.VMEM((8, 2, 8, 128), f32),
            pltpu.VMEM((2, 2, 2, 8, 128), f32),
            pltpu.VMEM((gx_count, kept, 128), f32),
            pltpu.VMEM((gx_count, kept, 128), f32),
            pltpu.VMEM((gx_count, kept, 128), f32),
            pltpu.VMEM((gx_count, kept, 128), f32),
            pltpu.VMEM((gx_count, kept, 16 * gy_count), f32),
            pltpu.VMEM((gx_count, kept, 16 * gy_count), f32),
            pltpu.VMEM((2, gx_count * kept, 128), f32),
            pltpu.VMEM((gy_count, kept, 512), f32),
            pltpu.VMEM((gy_count, kept, 512), f32),
            pltpu.VMEM((2, 4, 8, 128), f32),
            pltpu.VMEM((2, 2, 8, 128), f32),
        ]
        + [pltpu.VMEM(table.shape, table.dtype) for table in tables]
        + [
            dma((13,)),
            dma((2,)),
            dma((2,)),
            dma((8,)),
            dma((8,)),
            dma((gy_count,)),
            dma((gy_count,)),
            dma((gx_count,)),
            dma((gx_count,)),
            dma((gx_count,)),
            dma((gx_count,)),
            dma((gx_count,)),
            dma((gx_count,)),
            dma((gy_count,)),
            dma((gy_count,)),
        ],
        compiler_params=pltpu.CompilerParams(collective_id=0, has_side_effects=True),
    )(
        electric,
        magnetic,
        material,
        monitor_spectra,
        slab_spectra,
        *[jnp.asarray(table) for table in tables],
        permittivity,
        wave_index,
        jnp.asarray(monitor_weights(freq_count)),
        jnp.asarray(slab_weights(freq_count)),
    )
    electric_next, magnetic_next, slab_next, monitor_next, orders = pl.pallas_call(
        hand_over_kernel,
        name="hand_over",
        out_shape=tuple(jax.ShapeDtypeStruct(value.shape, f32) for value in held),
        in_specs=[vmem] * 5,
        out_specs=(hbm,) * 5,
        scratch_shapes=[dma((5,))],
    )(*[pltpu.with_memory_space_constraint(value, pltpu.VMEM) for value in held])
    return (
        electric_next,
        magnetic_next,
        slab_next,
        monitor_next,
        orders,
    )


def solution(mesh, order_count=128):
    fields = P(None, None, "gx", "gy")
    spectra = P(None, None, None, "gx", "gy")
    return jax.shard_map(
        functools.partial(per_device, mesh.shape["gx"], mesh.shape["gy"], order_count),
        mesh=mesh,
        in_specs=(fields, fields, P(None, "gx", "gy"), P(), fields, spectra, P()),
        out_specs=(fields, fields, fields, spectra, P("gy", None, None, "gx", None)),
        check_vma=False,
    )
```

```python
import functools
import math

import jax
import jax.numpy as jnp
import numpy as np
from jax import lax
from jax.experimental import pallas as pl
from jax.experimental.pallas import tpu as pltpu
from jax.sharding import PartitionSpec as P

MESH = pl.DeviceIdType.MESH
OX = 64
TIME_STEP = 0.5
OMEGA_LOW = 0.15
OMEGA_HIGH = 0.8
EDGE_MOVES = ((0, -1), (0, 1), (-1, 0), (1, 0), (-1, -1), (1, -1), (-1, 1), (1, 1))


def omegas(freq_count):
    low, high = np.float32(OMEGA_LOW), np.float32(OMEGA_HIGH - OMEGA_LOW)
    return low + high * np.arange(freq_count, dtype=np.float32) / np.float32(freq_count - 1)


def slab_weights(freq_count):
    rows = []
    for step in (1, 2):
        angle = (np.float32(TIME_STEP * step) * omegas(freq_count)).astype(np.float64)
        rows.append(np.concatenate([TIME_STEP * np.cos(angle), -TIME_STEP * np.sin(angle)]))
    return np.stack(rows).astype(np.float32)


def monitor_weights(freq_count):
    rows = []
    for step in (1, 2):
        for lag in (0.0, 0.5):
            angle = (np.float32(TIME_STEP * (step - lag)) * omegas(freq_count)).astype(np.float64)
            rows += [TIME_STEP * np.cos(angle), -TIME_STEP * np.sin(angle)]
    return np.stack(rows).astype(np.float32)


def split_table(table):
    table = table.astype(np.float32)
    lead = table.astype(jnp.bfloat16)
    rest = (table - lead.astype(np.float32)).astype(jnp.bfloat16)
    return np.concatenate([lead, lead], axis=0), rest


def y_tables(gy_count, local_y, order_count):
    length = gy_count * local_y
    orders = np.arange(order_count) - order_count // 2
    inside = 2.0 * np.pi / length * (np.arange(local_y)[:, None] * orders[None, :] % length)
    blocks = 2.0 * np.pi / length * (local_y * np.arange(gy_count)[:, None] * orders[None, :] % length)
    local = np.concatenate([np.cos(inside), np.sin(inside)], axis=1)
    turn = np.stack([np.cos(blocks), np.sin(blocks)], axis=1)
    return split_table(local), turn.astype(np.float32)


def x_local_table(gx_count, local_x, components, full_length):
    length = gx_count * local_x
    orders = np.arange(OX) - OX // 2
    inside = 2.0 * np.pi / length * (np.arange(local_x)[:, None] * orders[None, :] % length)
    scale = 1.0 / math.sqrt(length * full_length)
    cosine, sine = np.cos(inside) * scale, np.sin(inside) * scale
    half, wide = components * local_x, components * OX
    local = np.zeros((128, 2 * wide))
    for c in range(components):
        real = slice(c * local_x, (c + 1) * local_x)
        imag = slice(half + c * local_x, half + (c + 1) * local_x)
        to_real = slice(c * OX, (c + 1) * OX)
        to_imag = slice(wide + c * OX, wide + (c + 1) * OX)
        local[real, to_real], local[real, to_imag] = cosine, -sine
        local[imag, to_real], local[imag, to_imag] = sine, cosine
    return split_table(local)


def x_turn_table(gx_count, local_x, kept):
    length = gx_count * local_x
    orders = np.arange(OX) - OX // 2
    blocks = 2.0 * np.pi / length * (local_x * np.arange(gx_count)[:, None] * orders[None, :] % length)
    turn = np.repeat(np.stack([np.cos(blocks), np.sin(blocks)]), kept, axis=1)
    return np.tile(turn, (1, 1, 2)).astype(np.float32)


def split_dot(value, table, rest):
    lead = value.astype(jnp.bfloat16)
    low = (value - lead.astype(jnp.float32)).astype(jnp.bfloat16)
    return jnp.dot(
        jnp.concatenate([lead, low], axis=1), table, preferred_element_type=jnp.float32
    ) + jnp.dot(lead, rest, preferred_element_type=jnp.float32)


def whole_kernel(
    gx_count,
    gy_count,
    electric,
    magnetic,
    material,
    monitor,
    slab,
    y_lead_in,
    y_rest_in,
    y_turn_in,
    xm_lead_in,
    xm_rest_in,
    xf_lead_in,
    xf_rest_in,
    x_turn_in,
    permittivity,
    wave_index,
    weights,
    slab_table,
    electric_out,
    magnetic_out,
    slab_out,
    monitor_out,
    orders_out,
    field,
    strip,
    classes,
    mbuf,
    rbuf,
    corner,
    edges,
    edges_in,
    edges_x,
    kbuf_m,
    kin_m,
    kbuf_f,
    kin_f,
    kbuf_h,
    kin_h,
    xbuf,
    share,
    share_in,
    records,
    slab_records,
    y_lead,
    y_rest,
    y_turn,
    xm_lead,
    xm_rest,
    xf_lead,
    xf_rest,
    x_turn,
    load_sem,
    strip_send,
    strip_recv,
    edge_send,
    edge_recv,
    a_send,
    a_recv,
    m_send,
    m_recv,
    f_send,
    f_recv,
    h_send,
    h_recv,
    c_send,
    c_recv,
):
    gx = lax.axis_index("gx")
    gy = lax.axis_index("gy")
    zi = gy // 2
    upper_half = gy - 2 * zi
    z_count = gy_count // 2
    kept = kbuf_m.shape[2]
    order_count = gx_count * kept

    def along_gx(step):
        return lax.rem(gx + (step + gx_count), gx_count)

    def along_gy(step):
        return lax.rem(gy + (step + gy_count), gy_count)

    loads = [
        pltpu.make_async_copy(source, target, load_sem.at[i])
        for i, (source, target) in enumerate(
            (
                (material, classes),
                (electric, field.at[0:3, 1:17, 0:8, :]),
                (magnetic, field.at[3:6, 1:17, 0:8, :]),
                (monitor, mbuf),
                (slab, slab_out),
                (y_lead_in, y_lead),
                (y_rest_in, y_rest),
                (y_turn_in, y_turn),
                (xm_lead_in, xm_lead),
                (xm_rest_in, xm_rest),
                (xf_lead_in, xf_lead),
                (xf_rest_in, xf_rest),
                (x_turn_in, x_turn),
            )
        )
    ]
    for load in loads:
        load.start()

    barrier = pltpu.get_barrier_semaphore()

    def greet_x(step, carry):
        pl.semaphore_signal(barrier, inc=1, device_id=(along_gx(step), gy), device_id_type=MESH)
        return carry

    def greet_twin(step, carry):
        pl.semaphore_signal(
            barrier, inc=1, device_id=(along_gx(step), 4 * zi + 1 - gy), device_id_type=MESH
        )
        return carry

    def greet_y(step, carry):
        pl.semaphore_signal(barrier, inc=1, device_id=(gx, along_gy(step)), device_id_type=MESH)
        return carry

    lax.fori_loop(1, gx_count, greet_x, 0)
    lax.fori_loop(1, gy_count, greet_y, 0)
    lax.fori_loop(1, gx_count, greet_twin, 0)
    for dx, dy in EDGE_MOVES[4:]:
        pl.semaphore_signal(
            barrier, inc=1, device_id=(along_gx(dx), along_gy(dy)), device_id_type=MESH
        )

    field[0:6, 0] = jnp.zeros((6, 16, 128), jnp.float32)
    field[0:6, 17] = jnp.zeros((6, 16, 128), jnp.float32)

    loads[0].wait()
    inverses = [1.0 / jnp.full((8, 128), permittivity[i], jnp.float32) for i in range(4)]
    for z in range(16):
        here = classes[z]
        value = jnp.zeros((8, 128), jnp.float32)
        for i in range(4):
            value = value + jnp.where(here == i, inverses[i], 0.0)
        field[6, z + 1, 0:8, :] = value
    loads[1].wait()
    loads[2].wait()

    lane = lax.broadcasted_iota(jnp.int32, (8, 128), 1)
    top = lax.broadcasted_iota(jnp.int32, (8, 128), 0) < 4
    cell = lax.rem(lane, 8)

    def pack(c, carry):
        held = jnp.zeros((8, 128), jnp.float32)
        for z in range(16):
            tile = field[c, z + 1, 0:8, :]
            held = jnp.where(lane // 8 == z, pltpu.roll(tile, (8 * z + 2) % 128, 1), held)
        corner[c] = held
        return carry

    lax.fori_loop(0, 7, pack, 0)

    for t in range(2):
        for side in range(2):
            held = jnp.zeros((8, 128), jnp.float32)
            for i in range(4 - t):
                moved = pltpu.roll(corner[4 * t + i], (2 * i - 2 * side) % 128, 1)
                held = jnp.where(cell // 2 == i, moved, held)
            edges[side, t] = held
    loads[3].wait()

    pl.semaphore_wait(barrier, 2 * (gx_count - 1) + gy_count - 1 + 4)

    shares = []
    for i, (dx, dy) in enumerate(EDGE_MOVES):
        if dy:
            source, target = edges.at[(1 - dy) // 2], edges_in.at[i]
        else:
            source, target = edges, edges_x.at[(1 + dx) // 2]
        shares.append(
            pltpu.make_async_remote_copy(
                src_ref=source,
                dst_ref=target,
                send_sem=edge_send.at[i],
                recv_sem=edge_recv.at[i],
                device_id=(along_gx(dx), along_gy(dy)),
                device_id_type=MESH,
            )
        )
    strips = []
    for i, (step, first, landing) in enumerate(((-1, 0, 8), (1, 6, 14))):
        strips.append(
            pltpu.make_async_remote_copy(
                src_ref=field.at[:, 1:17, first : first + 2, :],
                dst_ref=field.at[:, 1:17, landing : landing + 2, :],
                send_sem=strip_send.at[i],
                recv_sem=strip_recv.at[i],
                device_id=(along_gx(step), gy),
                device_id_type=MESH,
            )
        )
    for copy in shares[::-1] + strips:
        copy.start()

    def along_z(step):
        return lax.rem(zi + (step + z_count), z_count)

    def a_copy(to, own, slot):
        return pltpu.make_async_remote_copy(
            src_ref=mbuf.at[pl.ds(2 * to, 2), :, 0:3],
            dst_ref=rbuf.at[own],
            send_sem=a_send.at[slot],
            recv_sem=a_recv.at[own],
            device_id=(gx, 2 * to + upper_half),
            device_id_type=MESH,
        )

    def far_first(count):
        half = count // 2
        order = [half]
        for i in range(1, half):
            order += [half - i, half + i]
        return order

    for step in far_first(z_count):
        a_copy(along_z(step), zi, step).start()

    def own_turn(re, im, b):
        turn = y_turn[b]
        cosine, sine = turn[0:1, :], turn[1:2, :]
        return re * cosine + im * sine, im * cosine - re * sine

    def x_copy(source, target, send_sem, recv_sem, g, own, slot):
        return pltpu.make_async_remote_copy(
            src_ref=source.at[g],
            dst_ref=target.at[own],
            send_sem=send_sem.at[slot],
            recv_sem=recv_sem.at[own],
            device_id=(g, gy),
            device_id_type=MESH,
        )

    def send_x(*kind):
        def body(step, carry):
            x_copy(*kind, along_gx(step), gx, step).start()
            return carry

        lax.fori_loop(1, gx_count, body, 0)
        source, target = kind[:2]
        target[gx] = source[gx]

    def take_x(*kind):
        def body(step, carry):
            x_copy(*kind, along_gx(step), along_gx(-step), step).wait_recv()
            return carry

        lax.fori_loop(1, gx_count, body, 0)

    for load in loads[5:8]:
        load.wait()
    for q in range(gy_count // 8):
        rows = [mbuf[w, part, 3] for part in range(2) for w in range(8 * q, 8 * q + 8)]
        product = split_dot(jnp.concatenate(rows, axis=0), y_lead[...], y_rest[...])
        a, b = product[0:64], product[64:128]
        re, im = own_turn(
            a[:, 0:order_count] + b[:, order_count:], b[:, 0:order_count] - a[:, order_count:], gy
        )
        turned = jnp.transpose(jnp.concatenate([re, im], axis=0))
        for g in range(gx_count):
            kbuf_h[g, :, 128 * q : 128 * (q + 1)] = turned[kept * g : kept * (g + 1), :]
    send_x(kbuf_h, kin_h, h_send, h_recv)

    for copy in shares:
        copy.wait_recv()

    for c in range(7):
        t, i = c // 4, c % 4

        def shifted(value, to):
            return pltpu.roll(value, (to - 2 * i) % 128, 1)

        behind, ahead = shifted(edges_in[1, t], 0), shifted(edges_in[0, t], 6)
        own = corner[c]
        strip[c, 0:8] = jnp.where(
            cell < 4,
            jnp.where(cell < 2, behind, own),
            jnp.where(cell < 6, pltpu.roll(own, 4, 1), ahead),
        )
        behind = shifted(jnp.where(top, edges_in[6, t], edges_in[7, t]), 0)
        ahead = shifted(jnp.where(top, edges_in[4, t], edges_in[5, t]), 6)
        near_last = shifted(jnp.where(top, edges_x[0, 0, t], edges_x[1, 0, t]), 4)
        near_first = shifted(jnp.where(top, edges_x[0, 1, t], edges_x[1, 1, t]), 2)
        strip[c, 8:16] = jnp.where(
            cell < 4,
            jnp.where(cell < 2, behind, near_first),
            jnp.where(cell < 6, near_last, ahead),
        )
    for copy in strips:
        copy.wait()

    wide_lane = lax.broadcasted_iota(jnp.int32, (16, 128), 1)
    last_lane, first_lane = wide_lane == 127, wide_lane == 0
    last_layer, first_layer = wide_lane >= 120, wide_lane < 8

    def x_ahead(value):
        return pltpu.roll(value, 15, 0)

    def x_behind(value):
        return pltpu.roll(value, 1, 0)

    def strip_h():
        ex, ey, ez = strip[0], strip[1], strip[2]
        ex_up = jnp.where(last_layer, 0.0, pltpu.roll(ex, 120, 1))
        ey_up = jnp.where(last_layer, 0.0, pltpu.roll(ey, 120, 1))
        ez_y, ex_y = pltpu.roll(ez, 127, 1), pltpu.roll(ex, 127, 1)
        strip[3] = strip[3] - TIME_STEP * (ez_y - ez - (ey_up - ey))
        strip[4] = strip[4] - TIME_STEP * ((ex_up - ex) - (x_ahead(ez) - ez))
        strip[5] = strip[5] - TIME_STEP * (x_ahead(ey) - ey - (ex_y - ex))

    def strip_e():
        hx, hy, hz = strip[3], strip[4], strip[5]
        hx_down = jnp.where(first_layer, 0.0, pltpu.roll(hx, 8, 1))
        hy_down = jnp.where(first_layer, 0.0, pltpu.roll(hy, 8, 1))
        hz_y, hx_y = pltpu.roll(hz, 1, 1), pltpu.roll(hx, 1, 1)
        rate = TIME_STEP * strip[6]
        strip[0] = strip[0] + rate * (hz - hz_y - (hy - hy_down))
        strip[1] = strip[1] + rate * ((hx - hx_down) - (hz - x_behind(hz)))
        strip[2] = strip[2] + rate * (hy - x_behind(hy) - (hx - hx_y))

    def main_h(z):
        def y_ahead(value, c):
            edge = pltpu.roll(strip[c], (129 - 8 * z), 1)
            return jnp.where(last_lane, edge, pltpu.roll(value, 127, 1))

        ex, ey, ez = field[0, z], field[1, z], field[2, z]
        ex_up, ey_up = field[0, z + 1], field[1, z + 1]
        field[3, z] = field[3, z] - TIME_STEP * (y_ahead(ez, 2) - ez - (ey_up - ey))
        field[4, z] = field[4, z] - TIME_STEP * ((ex_up - ex) - (x_ahead(ez) - ez))
        field[5, z] = field[5, z] - TIME_STEP * (x_ahead(ey) - ey - (y_ahead(ex, 0) - ex))

    def main_e(z):
        def y_behind(value, c):
            edge = pltpu.roll(strip[c], (135 - 8 * z) % 128, 1)
            return jnp.where(first_lane, edge, pltpu.roll(value, 1, 1))

        hx, hy, hz = field[3, z], field[4, z], field[5, z]
        hx_down, hy_down = field[3, z - 1], field[4, z - 1]
        rate = TIME_STEP * field[6, z]
        field[0, z] = field[0, z] + rate * (hz - y_behind(hz, 5) - (hy - hy_down))
        field[1, z] = field[1, z] + rate * ((hx - hx_down) - (hz - x_behind(hz)))
        field[2, z] = field[2, z] + rate * (hy - x_behind(hy) - (hx - y_behind(hx, 3)))

    def one_step(step, carry):
        for z in range(1, 17):
            main_h(z)
        strip_h()
        for z in range(1, 17):
            main_e(z)
        strip_e()
        for c in range(2):
            slab_records[c, step] = field[c, 9, 0:8, :]
        for c, row in enumerate((0, 1, 3, 4)):
            records[step, c] = field[row, 16, 0:8, :]
        return carry

    lax.fori_loop(0, 2, one_step, 0)

    for load in loads[8:]:
        load.wait()

    product = split_dot(records[...].reshape(64, 128), y_lead[...], y_rest[...])
    re, im = own_turn(product[:, 0:order_count], -product[:, order_count:], gy)
    turned = jnp.transpose(jnp.concatenate([re, im], axis=0))
    for g in range(gx_count):
        kbuf_f[g] = turned[kept * g : kept * (g + 1), :]

    send_x(kbuf_f, kin_f, f_send, f_recv)

    def hand_out(z, carry):
        for c in range(3):
            electric_out[c, z] = field[c, z + 1, 0:8, :]
            magnetic_out[c, z] = field[3 + c, z + 1, 0:8, :]
        return carry

    lax.fori_loop(0, 16, hand_out, 0)
    loads[4].wait()
    slab_held = [[slab_records[c, s] for s in range(2)] for c in range(2)]

    def slab_update(i, carry):
        for j in range(4):
            f = 4 * i + j
            first, second = slab_table[0, f], slab_table[1, f]
            for c in range(2):
                slab_out[c, f] = slab_out[c, f] + (
                    first * slab_held[c][0] + second * slab_held[c][1]
                )
        return carry

    lax.fori_loop(0, slab_out.shape[1] // 4, slab_update, 0)
    held = [[records[s, c] for c in range(4)] for s in range(2)]

    def weights_of(w):
        pick = wave_index[w]
        return [
            [[weights[4 * s + 2 * kind + i, pick] for i in range(2)] for kind in range(2)]
            for s in range(2)
        ]

    def monitor_update(w, carry):
        scale = weights_of(w)
        for i in range(2):
            for c in range(4):
                monitor_out[w, i, c] = mbuf[w, i, c] + (
                    scale[0][c // 2][i] * held[0][c] + scale[1][c // 2][i] * held[1][c]
                )
        return carry


    cosine, sine = x_turn[0], x_turn[1]

    def folded(value):
        total = value[0:8]
        for r in range(8, kept * gx_count, 8):
            total = total + value[r : r + 8]
        return total[0:kept] + total[kept : 2 * kept]

    def x_sums(values, lead, rest, blocks):
        product = split_dot(values, lead[...], rest[...])
        real, imag = [], []
        for j in range(blocks):
            re = product[:, 128 * j : 128 * (j + 1)]
            im = product[:, 128 * (blocks + j) : 128 * (blocks + j + 1)]
            real.append(folded(re * cosine + im * sine))
            imag.append(folded(im * cosine - re * sine))
        return real, imag

    def y_part(blocks, owners, sums):
        rows = jnp.concatenate([block.reshape(96, 128) for block in blocks], axis=0)
        product = split_dot(rows, y_lead[...], y_rest[...])
        for i, b in enumerate(owners):
            for u in range(2):
                first = 96 * i + 48 * u
                a, c = product[first : first + 24], product[first + 24 : first + 48]
                re = a[:, 0:order_count] + c[:, order_count:]
                im = c[:, 0:order_count] - a[:, order_count:]
                re, im = own_turn(re, im, b)
                sums[u] = (sums[u][0] + re, sums[u][1] + im)

    empty = jnp.zeros((24, order_count), jnp.float32)
    sums = [(empty, empty), (empty, empty)]
    arriving = [0] + far_first(z_count)[::-1]
    for i in range(0, z_count, 4):
        blocks, owners = [], []
        for step in arriving[i : i + 4]:
            source = along_z(-step)
            if step:
                a_copy(along_z(step), source, step).wait_recv()
                blocks.append(rbuf[source])
            else:
                blocks.append(mbuf[pl.ds(2 * zi, 2), :, 0:3])
            owners.append(2 * source + upper_half)
        y_part(blocks, owners, sums)

    spare = jnp.zeros((72, order_count), jnp.float32)
    for u in range(2):
        spectrum = jnp.concatenate([sums[u][0], spare[0:8], sums[u][1], spare], axis=0)
        turned = jnp.transpose(spectrum)
        for g in range(gx_count):
            kbuf_m[u, g] = turned[kept * g : kept * (g + 1), :]

    def m_copy(g, other, own, slot):
        half = upper_half + other - 2 * other * upper_half
        return pltpu.make_async_remote_copy(
            src_ref=kbuf_m.at[half, g],
            dst_ref=kin_m.at[upper_half, gx] if own is None else kin_m.at[half, own],
            send_sem=m_send.at[other, slot],
            recv_sem=m_recv.at[other, gx if own is None else own],
            device_id=(g, 2 * zi + half),
            device_id_type=MESH,
        )

    for other in (1, 0):

        def send_m(step, carry):
            m_copy(along_gx(step), other, None, step).start()
            return carry

        lax.fori_loop(1 - other, gx_count, send_m, 0)
    kin_m[upper_half, gx] = kbuf_m[upper_half, gx]

    upper = lax.broadcasted_iota(jnp.int32, (kept, 128), 1) >= OX
    take_x(kbuf_h, kin_h, h_send, h_recv)
    for q in range(gy_count // 8):
        for g in range(gx_count):
            xbuf[q, kept * g : kept * (g + 1), :] = kin_h[g, :, 128 * q : 128 * (q + 1)]
    for q in range(gy_count // 8):
        h_real, h_imag = x_sums(xbuf[q], xf_lead, xf_rest, 4)
        for j in range(8):
            for first, blocks in ((128, h_real), (384, h_imag)):
                block = blocks[j // 2]
                block = block if j % 2 else pltpu.roll(block, OX, 1)
                share[8 * q + j, :, first : first + 128] = jnp.where(upper, block, 0.0)

    take_x(kbuf_f, kin_f, f_send, f_recv)
    for g in range(gx_count):
        xbuf[0, kept * g : kept * (g + 1), :] = kin_f[g]
    f_real, f_imag = x_sums(xbuf[0], xf_lead, xf_rest, 4)

    def weigh(w, carry):
        scale = weights_of(w)
        for kind in range(2):
            (r0, i0), (r1, i1) = scale[0][kind], scale[1][kind]
            re0, im0, re1, im1 = f_real[kind], f_imag[kind], f_real[2 + kind], f_imag[2 + kind]
            real = (r0 * re0 - i0 * im0) + (r1 * re1 - i1 * im1)
            imag = (r0 * im0 + i0 * re0) + (r1 * im1 + i1 * re1)
            first, second = 128 * kind, 256 + 128 * kind
            if kind:
                real, imag = real + share[w, :, 128:256], imag + share[w, :, 384:512]
            share[w, :, first : first + 128] = real
            share[w, :, second : second + 128] = imag
        return carry

    lax.fori_loop(0, gy_count, weigh, 0)

    def c_copy(w, b, slot):
        return pltpu.make_async_remote_copy(
            src_ref=share.at[w],
            dst_ref=share_in.at[b],
            send_sem=c_send.at[slot],
            recv_sem=c_recv.at[b],
            device_id=(gx, w),
            device_id_type=MESH,
        )

    for step in far_first(gy_count):
        c_copy(along_gy(step), gy, step).start()
    lax.fori_loop(0, gy_count, monitor_update, 0)

    for other in (0, 1):

        def take_m(step, carry):
            m_copy(along_gx(step), other, along_gx(-step), step).wait_recv()
            return carry

        lax.fori_loop(1 - other, gx_count, take_m, 0)
    for g in range(gx_count):
        xbuf[1, kept * g : kept * (g + 1), :] = kin_m[0, g] + kin_m[1, g]
    m_real, m_imag = x_sums(xbuf[1], xm_lead, xm_rest, 2)
    total = share[gy]
    for step in far_first(gy_count)[::-1]:
        b = along_gy(-step)
        c_copy(along_gy(step), b, step).wait_recv()
        total = total + share_in[b]

    for part, blocks in enumerate((m_real, m_imag)):
        for kind in range(2):
            first = 128 * (2 * part + kind)
            value = total[:, first : first + 128] + blocks[kind]
            for c in range(2):
                orders_out[0, part, 2 * kind + c] = value[:, c * OX : (c + 1) * OX]

    for copy in shares:
        copy.wait_send()

    def sent_y(step, carry):
        c_copy(along_gy(step), gy, step).wait_send()
        return carry

    def sent_x(step, carry):
        x_copy(kbuf_f, kin_f, f_send, f_recv, along_gx(step), gx, step).wait_send()
        x_copy(kbuf_h, kin_h, h_send, h_recv, along_gx(step), gx, step).wait_send()
        return carry

    for step in range(1, z_count):
        a_copy(along_z(step), zi, step).wait_send()
    for other in (1, 0):

        def sent_m(step, carry):
            m_copy(along_gx(step), other, None, step).wait_send()
            return carry

        lax.fori_loop(1 - other, gx_count, sent_m, 0)
    lax.fori_loop(1, gy_count, sent_y, 0)
    lax.fori_loop(1, gx_count, sent_x, 0)


def hand_over_kernel(*refs):
    count = len(refs) // 2
    copies = [
        pltpu.make_async_copy(source, target, refs[-1].at[i])
        for i, (source, target) in enumerate(zip(refs[:count], refs[count:-1]))
    ]
    for copy in copies:
        copy.start()
    for copy in copies:
        copy.wait()


def per_device(
    gx_count,
    gy_count,
    order_count,
    electric,
    magnetic,
    material,
    permittivity,
    slab_spectra,
    monitor_spectra,
    wave_index,
):
    freq_count = slab_spectra.shape[1] // 2
    kept = order_count // gx_count
    (y_lead, y_rest), y_turn = y_tables(gy_count, 128, order_count)
    xm_lead, xm_rest = x_local_table(gx_count, 8, 4, gy_count * 128)
    xf_lead, xf_rest = x_local_table(gx_count, 8, 8, gy_count * 128)
    x_turn = x_turn_table(gx_count, 8, kept)
    tables = [y_lead, y_rest, y_turn, xm_lead, xm_rest, xf_lead, xf_rest, x_turn]
    hbm = pl.BlockSpec(memory_space=pl.ANY)
    vmem = pl.BlockSpec(memory_space=pltpu.VMEM)
    smem = pl.BlockSpec(memory_space=pltpu.SMEM)
    f32 = jnp.float32
    dma = pltpu.SemaphoreType.DMA
    held = pl.pallas_call(
        functools.partial(whole_kernel, gx_count, gy_count),
        name="leapfrog_orders",
        out_shape=(
            pltpu.VMEM(electric.shape, f32),
            pltpu.VMEM(magnetic.shape, f32),
            pltpu.VMEM(slab_spectra.shape, f32),
            pltpu.VMEM(monitor_spectra.shape, f32),
            pltpu.VMEM((1, 2, 4, kept, OX), f32),
        ),
        in_specs=[hbm] * 13 + [smem] * 4,
        out_specs=(vmem,) * 5,
        scratch_shapes=[
            pltpu.VMEM((7, 18, 16, 128), f32),
            pltpu.VMEM((7, 16, 128), f32),
            pltpu.VMEM((16, 8, 128), jnp.int32),
            pltpu.VMEM((gy_count, 2, 4, 8, 128), f32),
            pltpu.VMEM((gy_count // 2, 2, 2, 3, 8, 128), f32),
            pltpu.VMEM((7, 8, 128), f32),
            pltpu.VMEM((2, 2, 8, 128), f32),
            pltpu.VMEM((8, 2, 8, 128), f32),
            pltpu.VMEM((2, 2, 2, 8, 128), f32),
            pltpu.VMEM((2, gx_count, kept, 128), f32),
            pltpu.VMEM((2, gx_count, kept, 128), f32),
            pltpu.VMEM((gx_count, kept, 128), f32),
            pltpu.VMEM((gx_count, kept, 128), f32),
            pltpu.VMEM((gx_count, kept, 16 * gy_count), f32),
            pltpu.VMEM((gx_count, kept, 16 * gy_count), f32),
            pltpu.VMEM((2, gx_count * kept, 128), f32),
            pltpu.VMEM((gy_count, kept, 512), f32),
            pltpu.VMEM((gy_count, kept, 512), f32),
            pltpu.VMEM((2, 4, 8, 128), f32),
            pltpu.VMEM((2, 2, 8, 128), f32),
        ]
        + [pltpu.VMEM(table.shape, table.dtype) for table in tables]
        + [
            dma((13,)),
            dma((2,)),
            dma((2,)),
            dma((8,)),
            dma((8,)),
            dma((gy_count // 2,)),
            dma((gy_count // 2,)),
            dma((2, gx_count)),
            dma((2, gx_count)),
            dma((gx_count,)),
            dma((gx_count,)),
            dma((gx_count,)),
            dma((gx_count,)),
            dma((gy_count,)),
            dma((gy_count,)),
        ],
        compiler_params=pltpu.CompilerParams(collective_id=0, has_side_effects=True),
    )(
        electric,
        magnetic,
        material,
        monitor_spectra,
        slab_spectra,
        *[jnp.asarray(table) for table in tables],
        permittivity,
        wave_index,
        jnp.asarray(monitor_weights(freq_count)),
        jnp.asarray(slab_weights(freq_count)),
    )
    electric_next, magnetic_next, slab_next, monitor_next, orders = pl.pallas_call(
        hand_over_kernel,
        name="hand_over",
        out_shape=tuple(jax.ShapeDtypeStruct(value.shape, f32) for value in held),
        in_specs=[vmem] * 5,
        out_specs=(hbm,) * 5,
        scratch_shapes=[dma((5,))],
    )(*[pltpu.with_memory_space_constraint(value, pltpu.VMEM) for value in held])
    return (
        electric_next,
        magnetic_next,
        slab_next,
        monitor_next,
        orders,
    )


def solution(mesh, order_count=128):
    fields = P(None, None, "gx", "gy")
    spectra = P(None, None, None, "gx", "gy")
    return jax.shard_map(
        functools.partial(per_device, mesh.shape["gx"], mesh.shape["gy"], order_count),
        mesh=mesh,
        in_specs=(fields, fields, P(None, "gx", "gy"), P(), fields, spectra, P()),
        out_specs=(fields, fields, fields, spectra, P("gy", None, None, "gx", None)),
        check_vma=False,
    )
```

```python
import functools
import math

import jax
import jax.numpy as jnp
import numpy as np
from jax import lax
from jax.experimental import pallas as pl
from jax.experimental.pallas import tpu as pltpu
from jax.sharding import PartitionSpec as P

MESH = pl.DeviceIdType.MESH
OX = 64
TIME_STEP = 0.5
OMEGA_LOW = 0.15
OMEGA_HIGH = 0.8
EDGE_MOVES = ((0, -1), (0, 1), (-1, 0), (1, 0), (-1, -1), (1, -1), (-1, 1), (1, 1))


def omegas(freq_count):
    low, high = np.float32(OMEGA_LOW), np.float32(OMEGA_HIGH - OMEGA_LOW)
    return low + high * np.arange(freq_count, dtype=np.float32) / np.float32(freq_count - 1)


def slab_weights(freq_count):
    rows = []
    for step in (1, 2):
        angle = (np.float32(TIME_STEP * step) * omegas(freq_count)).astype(np.float64)
        rows.append(np.concatenate([TIME_STEP * np.cos(angle), -TIME_STEP * np.sin(angle)]))
    return np.stack(rows).astype(np.float32)


def monitor_weights(freq_count):
    rows = []
    for step in (1, 2):
        for lag in (0.0, 0.5):
            angle = (np.float32(TIME_STEP * (step - lag)) * omegas(freq_count)).astype(np.float64)
            rows += [TIME_STEP * np.cos(angle), -TIME_STEP * np.sin(angle)]
    return np.stack(rows).astype(np.float32)


def split_table(table):
    table = table.astype(np.float32)
    lead = table.astype(jnp.bfloat16)
    rest = (table - lead.astype(np.float32)).astype(jnp.bfloat16)
    return np.concatenate([lead, lead], axis=0), rest


def y_tables(gy_count, local_y, order_count):
    length = gy_count * local_y
    orders = np.arange(order_count) - order_count // 2
    inside = 2.0 * np.pi / length * (np.arange(local_y)[:, None] * orders[None, :] % length)
    blocks = 2.0 * np.pi / length * (local_y * np.arange(gy_count)[:, None] * orders[None, :] % length)
    local = np.concatenate([np.cos(inside), np.sin(inside)], axis=1)
    turn = np.stack([np.cos(blocks), np.sin(blocks)], axis=1)
    return split_table(local), turn.astype(np.float32)


def x_local_table(gx_count, local_x, components, full_length):
    length = gx_count * local_x
    orders = np.arange(OX) - OX // 2
    inside = 2.0 * np.pi / length * (np.arange(local_x)[:, None] * orders[None, :] % length)
    scale = 1.0 / math.sqrt(length * full_length)
    cosine, sine = np.cos(inside) * scale, np.sin(inside) * scale
    half, wide = components * local_x, components * OX
    local = np.zeros((128, 2 * wide))
    for c in range(components):
        real = slice(c * local_x, (c + 1) * local_x)
        imag = slice(half + c * local_x, half + (c + 1) * local_x)
        to_real = slice(c * OX, (c + 1) * OX)
        to_imag = slice(wide + c * OX, wide + (c + 1) * OX)
        local[real, to_real], local[real, to_imag] = cosine, -sine
        local[imag, to_real], local[imag, to_imag] = sine, cosine
    return split_table(local)


def x_turn_table(gx_count, local_x, kept):
    length = gx_count * local_x
    orders = np.arange(OX) - OX // 2
    blocks = 2.0 * np.pi / length * (local_x * np.arange(gx_count)[:, None] * orders[None, :] % length)
    turn = np.repeat(np.stack([np.cos(blocks), np.sin(blocks)]), kept, axis=1)
    return np.tile(turn, (1, 1, 2)).astype(np.float32)


def split_dot(value, table, rest):
    lead = value.astype(jnp.bfloat16)
    low = (value - lead.astype(jnp.float32)).astype(jnp.bfloat16)
    return jnp.dot(
        jnp.concatenate([lead, low], axis=1), table, preferred_element_type=jnp.float32
    ) + jnp.dot(lead, rest, preferred_element_type=jnp.float32)


def whole_kernel(
    gx_count,
    gy_count,
    electric,
    magnetic,
    material,
    monitor,
    slab,
    y_lead_in,
    y_rest_in,
    y_turn_in,
    xm_lead_in,
    xm_rest_in,
    xf_lead_in,
    xf_rest_in,
    x_turn_in,
    permittivity,
    wave_index,
    weights,
    slab_table,
    electric_out,
    magnetic_out,
    slab_out,
    monitor_out,
    orders_out,
    field,
    strip,
    classes,
    mbuf,
    rbuf,
    corner,
    edges,
    edges_in,
    edges_x,
    kbuf_m,
    kin_m,
    kbuf_f,
    kin_f,
    kbuf_h,
    kin_h,
    xbuf,
    share,
    share_in,
    records,
    slab_records,
    y_lead,
    y_rest,
    y_turn,
    xm_lead,
    xm_rest,
    xf_lead,
    xf_rest,
    x_turn,
    load_sem,
    strip_send,
    strip_recv,
    edge_send,
    edge_recv,
    a_send,
    a_recv,
    m_send,
    m_recv,
    f_send,
    f_recv,
    h_send,
    h_recv,
    c_send,
    c_recv,
):
    gx = lax.axis_index("gx")
    gy = lax.axis_index("gy")
    zi = gy // 2
    upper_half = gy - 2 * zi
    z_count = gy_count // 2
    kept = kbuf_m.shape[2]
    order_count = gx_count * kept

    def along_gx(step):
        return lax.rem(gx + (step + gx_count), gx_count)

    def along_gy(step):
        return lax.rem(gy + (step + gy_count), gy_count)

    loads = [
        pltpu.make_async_copy(source, target, load_sem.at[i])
        for i, (source, target) in enumerate(
            (
                (material, classes),
                (electric, field.at[0:3, 1:17, 0:8, :]),
                (magnetic, field.at[3:6, 1:17, 0:8, :]),
                (monitor, mbuf),
                (slab, slab_out),
                (y_lead_in, y_lead),
                (y_rest_in, y_rest),
                (y_turn_in, y_turn),
                (xm_lead_in, xm_lead),
                (xm_rest_in, xm_rest),
                (xf_lead_in, xf_lead),
                (xf_rest_in, xf_rest),
                (x_turn_in, x_turn),
            )
        )
    ]
    for load in loads:
        load.start()

    barrier = pltpu.get_barrier_semaphore()

    def greet_x(step, carry):
        pl.semaphore_signal(barrier, inc=1, device_id=(along_gx(step), gy), device_id_type=MESH)
        return carry

    def greet_twin(step, carry):
        pl.semaphore_signal(
            barrier, inc=1, device_id=(along_gx(step), 4 * zi + 1 - gy), device_id_type=MESH
        )
        return carry

    def greet_y(step, carry):
        pl.semaphore_signal(barrier, inc=1, device_id=(gx, along_gy(step)), device_id_type=MESH)
        return carry

    lax.fori_loop(1, gx_count, greet_x, 0)
    lax.fori_loop(1, gy_count, greet_y, 0)
    lax.fori_loop(1, gx_count, greet_twin, 0)
    for dx, dy in EDGE_MOVES[4:]:
        pl.semaphore_signal(
            barrier, inc=1, device_id=(along_gx(dx), along_gy(dy)), device_id_type=MESH
        )

    field[0:6, 0] = jnp.zeros((6, 16, 128), jnp.float32)
    field[0:6, 17] = jnp.zeros((6, 16, 128), jnp.float32)

    loads[0].wait()
    inverses = [1.0 / jnp.full((8, 128), permittivity[i], jnp.float32) for i in range(4)]
    for z in range(16):
        here = classes[z]
        value = jnp.zeros((8, 128), jnp.float32)
        for i in range(4):
            value = value + jnp.where(here == i, inverses[i], 0.0)
        field[6, z + 1, 0:8, :] = value
    loads[1].wait()
    loads[2].wait()

    lane = lax.broadcasted_iota(jnp.int32, (8, 128), 1)
    top = lax.broadcasted_iota(jnp.int32, (8, 128), 0) < 4
    cell = lax.rem(lane, 8)

    def pack(c, carry):
        held = jnp.zeros((8, 128), jnp.float32)
        for z in range(16):
            tile = field[c, z + 1, 0:8, :]
            held = jnp.where(lane // 8 == z, pltpu.roll(tile, (8 * z + 2) % 128, 1), held)
        corner[c] = held
        return carry

    lax.fori_loop(0, 7, pack, 0)

    for t in range(2):
        for side in range(2):
            held = jnp.zeros((8, 128), jnp.float32)
            for i in range(4 - t):
                moved = pltpu.roll(corner[4 * t + i], (2 * i - 2 * side) % 128, 1)
                held = jnp.where(cell // 2 == i, moved, held)
            edges[side, t] = held
    loads[3].wait()

    pl.semaphore_wait(barrier, 2 * (gx_count - 1) + gy_count - 1 + 4)

    shares = []
    for i, (dx, dy) in enumerate(EDGE_MOVES):
        if dy:
            source, target = edges.at[(1 - dy) // 2], edges_in.at[i]
        else:
            source, target = edges, edges_x.at[(1 + dx) // 2]
        shares.append(
            pltpu.make_async_remote_copy(
                src_ref=source,
                dst_ref=target,
                send_sem=edge_send.at[i],
                recv_sem=edge_recv.at[i],
                device_id=(along_gx(dx), along_gy(dy)),
                device_id_type=MESH,
            )
        )
    strips = []
    for i, (step, first, landing) in enumerate(((-1, 0, 8), (1, 6, 14))):
        strips.append(
            pltpu.make_async_remote_copy(
                src_ref=field.at[:, 1:17, first : first + 2, :],
                dst_ref=field.at[:, 1:17, landing : landing + 2, :],
                send_sem=strip_send.at[i],
                recv_sem=strip_recv.at[i],
                device_id=(along_gx(step), gy),
                device_id_type=MESH,
            )
        )
    for copy in shares[::-1] + strips:
        copy.start()

    def along_z(step):
        return lax.rem(zi + (step + z_count), z_count)

    def a_copy(to, own, slot):
        return pltpu.make_async_remote_copy(
            src_ref=mbuf.at[pl.ds(2 * to, 2), :, 0:3],
            dst_ref=rbuf.at[own],
            send_sem=a_send.at[slot],
            recv_sem=a_recv.at[own],
            device_id=(gx, 2 * to + upper_half),
            device_id_type=MESH,
        )

    def far_first(count):
        half = count // 2
        order = [half]
        for i in range(1, half):
            order += [half - i, half + i]
        return order

    for step in far_first(z_count):
        a_copy(along_z(step), zi, step).start()

    def own_turn(re, im, b):
        turn = y_turn[b]
        cosine, sine = turn[0:1, :], turn[1:2, :]
        return re * cosine + im * sine, im * cosine - re * sine

    def x_copy(source, target, send_sem, recv_sem, g, own, slot):
        return pltpu.make_async_remote_copy(
            src_ref=source.at[g],
            dst_ref=target.at[own],
            send_sem=send_sem.at[slot],
            recv_sem=recv_sem.at[own],
            device_id=(g, gy),
            device_id_type=MESH,
        )

    def send_x(*kind):
        def body(step, carry):
            x_copy(*kind, along_gx(step), gx, step).start()
            return carry

        lax.fori_loop(1, gx_count, body, 0)
        source, target = kind[:2]
        target[gx] = source[gx]

    def take_x(*kind):
        def body(step, carry):
            x_copy(*kind, along_gx(step), along_gx(-step), step).wait_recv()
            return carry

        lax.fori_loop(1, gx_count, body, 0)

    for load in loads[5:8]:
        load.wait()
    for q in range(gy_count // 8):
        rows = [mbuf[w, part, 3] for part in range(2) for w in range(8 * q, 8 * q + 8)]
        product = split_dot(jnp.concatenate(rows, axis=0), y_lead[...], y_rest[...])
        a, b = product[0:64], product[64:128]
        re, im = own_turn(
            a[:, 0:order_count] + b[:, order_count:], b[:, 0:order_count] - a[:, order_count:], gy
        )
        turned = jnp.transpose(jnp.concatenate([re, im], axis=0))
        for g in range(gx_count):
            kbuf_h[g, :, 128 * q : 128 * (q + 1)] = turned[kept * g : kept * (g + 1), :]
    send_x(kbuf_h, kin_h, h_send, h_recv)

    for copy in shares:
        copy.wait_recv()

    for c in range(7):
        t, i = c // 4, c % 4

        def shifted(value, to):
            return pltpu.roll(value, (to - 2 * i) % 128, 1)

        behind, ahead = shifted(edges_in[1, t], 0), shifted(edges_in[0, t], 6)
        own = corner[c]
        strip[c, 0:8] = jnp.where(
            cell < 4,
            jnp.where(cell < 2, behind, own),
            jnp.where(cell < 6, pltpu.roll(own, 4, 1), ahead),
        )
        behind = shifted(jnp.where(top, edges_in[6, t], edges_in[7, t]), 0)
        ahead = shifted(jnp.where(top, edges_in[4, t], edges_in[5, t]), 6)
        near_last = shifted(jnp.where(top, edges_x[0, 0, t], edges_x[1, 0, t]), 4)
        near_first = shifted(jnp.where(top, edges_x[0, 1, t], edges_x[1, 1, t]), 2)
        strip[c, 8:16] = jnp.where(
            cell < 4,
            jnp.where(cell < 2, behind, near_first),
            jnp.where(cell < 6, near_last, ahead),
        )
    for copy in strips:
        copy.wait()

    wide_lane = lax.broadcasted_iota(jnp.int32, (16, 128), 1)
    last_lane, first_lane = wide_lane == 127, wide_lane == 0
    last_layer, first_layer = wide_lane >= 120, wide_lane < 8

    def x_ahead(value):
        return pltpu.roll(value, 15, 0)

    def x_behind(value):
        return pltpu.roll(value, 1, 0)

    def strip_h():
        ex, ey, ez = strip[0], strip[1], strip[2]
        ex_up = jnp.where(last_layer, 0.0, pltpu.roll(ex, 120, 1))
        ey_up = jnp.where(last_layer, 0.0, pltpu.roll(ey, 120, 1))
        ez_y, ex_y = pltpu.roll(ez, 127, 1), pltpu.roll(ex, 127, 1)
        strip[3] = strip[3] - TIME_STEP * (ez_y - ez - (ey_up - ey))
        strip[4] = strip[4] - TIME_STEP * ((ex_up - ex) - (x_ahead(ez) - ez))
        strip[5] = strip[5] - TIME_STEP * (x_ahead(ey) - ey - (ex_y - ex))

    def strip_e():
        hx, hy, hz = strip[3], strip[4], strip[5]
        hx_down = jnp.where(first_layer, 0.0, pltpu.roll(hx, 8, 1))
        hy_down = jnp.where(first_layer, 0.0, pltpu.roll(hy, 8, 1))
        hz_y, hx_y = pltpu.roll(hz, 1, 1), pltpu.roll(hx, 1, 1)
        rate = TIME_STEP * strip[6]
        strip[0] = strip[0] + rate * (hz - hz_y - (hy - hy_down))
        strip[1] = strip[1] + rate * ((hx - hx_down) - (hz - x_behind(hz)))
        strip[2] = strip[2] + rate * (hy - x_behind(hy) - (hx - hx_y))

    def main_h(z):
        def y_ahead(value, c):
            edge = pltpu.roll(strip[c], (129 - 8 * z), 1)
            return jnp.where(last_lane, edge, pltpu.roll(value, 127, 1))

        ex, ey, ez = field[0, z], field[1, z], field[2, z]
        ex_up, ey_up = field[0, z + 1], field[1, z + 1]
        field[3, z] = field[3, z] - TIME_STEP * (y_ahead(ez, 2) - ez - (ey_up - ey))
        field[4, z] = field[4, z] - TIME_STEP * ((ex_up - ex) - (x_ahead(ez) - ez))
        field[5, z] = field[5, z] - TIME_STEP * (x_ahead(ey) - ey - (y_ahead(ex, 0) - ex))

    def main_e(z):
        def y_behind(value, c):
            edge = pltpu.roll(strip[c], (135 - 8 * z) % 128, 1)
            return jnp.where(first_lane, edge, pltpu.roll(value, 1, 1))

        hx, hy, hz = field[3, z], field[4, z], field[5, z]
        hx_down, hy_down = field[3, z - 1], field[4, z - 1]
        rate = TIME_STEP * field[6, z]
        field[0, z] = field[0, z] + rate * (hz - y_behind(hz, 5) - (hy - hy_down))
        field[1, z] = field[1, z] + rate * ((hx - hx_down) - (hz - x_behind(hz)))
        field[2, z] = field[2, z] + rate * (hy - x_behind(hy) - (hx - y_behind(hx, 3)))

    def one_step(step, carry):
        for z in range(1, 17):
            main_h(z)
        strip_h()
        for z in range(1, 17):
            main_e(z)
        strip_e()
        for c in range(2):
            slab_records[c, step] = field[c, 9, 0:8, :]
        for c, row in enumerate((0, 1, 3, 4)):
            records[step, c] = field[row, 16, 0:8, :]
        return carry

    lax.fori_loop(0, 2, one_step, 0)

    for load in loads[8:]:
        load.wait()

    product = split_dot(records[...].reshape(64, 128), y_lead[...], y_rest[...])
    re, im = own_turn(product[:, 0:order_count], -product[:, order_count:], gy)
    turned = jnp.transpose(jnp.concatenate([re, im], axis=0))
    for g in range(gx_count):
        kbuf_f[g] = turned[kept * g : kept * (g + 1), :]

    send_x(kbuf_f, kin_f, f_send, f_recv)

    held = [[records[s, c] for c in range(4)] for s in range(2)]

    def weights_of(w):
        pick = wave_index[w]
        return [
            [[weights[4 * s + 2 * kind + i, pick] for i in range(2)] for kind in range(2)]
            for s in range(2)
        ]

    def monitor_update(w, carry):
        scale = weights_of(w)
        for i in range(2):
            for c in range(4):
                monitor_out[w, i, c] = mbuf[w, i, c] + (
                    scale[0][c // 2][i] * held[0][c] + scale[1][c // 2][i] * held[1][c]
                )
        return carry


    cosine, sine = x_turn[0], x_turn[1]

    def folded(value):
        total = value[0:8]
        for r in range(8, kept * gx_count, 8):
            total = total + value[r : r + 8]
        return total[0:kept] + total[kept : 2 * kept]

    def x_sums(values, lead, rest, blocks):
        product = split_dot(values, lead[...], rest[...])
        real, imag = [], []
        for j in range(blocks):
            re = product[:, 128 * j : 128 * (j + 1)]
            im = product[:, 128 * (blocks + j) : 128 * (blocks + j + 1)]
            real.append(folded(re * cosine + im * sine))
            imag.append(folded(im * cosine - re * sine))
        return real, imag

    upper = lax.broadcasted_iota(jnp.int32, (kept, 128), 1) >= OX
    take_x(kbuf_h, kin_h, h_send, h_recv)
    for q in range(gy_count // 8):
        for g in range(gx_count):
            xbuf[q, kept * g : kept * (g + 1), :] = kin_h[g, :, 128 * q : 128 * (q + 1)]
    for q in range(gy_count // 8):
        h_real, h_imag = x_sums(xbuf[q], xf_lead, xf_rest, 4)
        for j in range(8):
            for first, blocks in ((128, h_real), (384, h_imag)):
                block = blocks[j // 2]
                block = block if j % 2 else pltpu.roll(block, OX, 1)
                share[8 * q + j, :, first : first + 128] = jnp.where(upper, block, 0.0)

    def y_part(blocks, owners, sums):
        rows = jnp.concatenate([block.reshape(96, 128) for block in blocks], axis=0)
        product = split_dot(rows, y_lead[...], y_rest[...])
        for i, b in enumerate(owners):
            for u in range(2):
                first = 96 * i + 48 * u
                a, c = product[first : first + 24], product[first + 24 : first + 48]
                re = a[:, 0:order_count] + c[:, order_count:]
                im = c[:, 0:order_count] - a[:, order_count:]
                re, im = own_turn(re, im, b)
                sums[u] = (sums[u][0] + re, sums[u][1] + im)

    empty = jnp.zeros((24, order_count), jnp.float32)
    sums = [(empty, empty), (empty, empty)]
    arriving = [0] + far_first(z_count)[::-1]
    for i in range(0, z_count, 4):
        blocks, owners = [], []
        for step in arriving[i : i + 4]:
            source = along_z(-step)
            if step:
                a_copy(along_z(step), source, step).wait_recv()
                blocks.append(rbuf[source])
            else:
                blocks.append(mbuf[pl.ds(2 * zi, 2), :, 0:3])
            owners.append(2 * source + upper_half)
        y_part(blocks, owners, sums)

    spare = jnp.zeros((72, order_count), jnp.float32)
    for u in range(2):
        spectrum = jnp.concatenate([sums[u][0], spare[0:8], sums[u][1], spare], axis=0)
        turned = jnp.transpose(spectrum)
        for g in range(gx_count):
            kbuf_m[u, g] = turned[kept * g : kept * (g + 1), :]

    def m_copy(g, other, own, slot):
        half = upper_half + other - 2 * other * upper_half
        return pltpu.make_async_remote_copy(
            src_ref=kbuf_m.at[half, g],
            dst_ref=kin_m.at[upper_half, gx] if own is None else kin_m.at[half, own],
            send_sem=m_send.at[other, slot],
            recv_sem=m_recv.at[other, gx if own is None else own],
            device_id=(g, 2 * zi + half),
            device_id_type=MESH,
        )

    for other in (1, 0):

        def send_m(step, carry):
            m_copy(along_gx(step), other, None, step).start()
            return carry

        lax.fori_loop(1 - other, gx_count, send_m, 0)
    kin_m[upper_half, gx] = kbuf_m[upper_half, gx]

    take_x(kbuf_f, kin_f, f_send, f_recv)
    for g in range(gx_count):
        xbuf[0, kept * g : kept * (g + 1), :] = kin_f[g]
    f_real, f_imag = x_sums(xbuf[0], xf_lead, xf_rest, 4)

    def weigh(w, carry):
        scale = weights_of(w)
        for kind in range(2):
            (r0, i0), (r1, i1) = scale[0][kind], scale[1][kind]
            re0, im0, re1, im1 = f_real[kind], f_imag[kind], f_real[2 + kind], f_imag[2 + kind]
            real = (r0 * re0 - i0 * im0) + (r1 * re1 - i1 * im1)
            imag = (r0 * im0 + i0 * re0) + (r1 * im1 + i1 * re1)
            first, second = 128 * kind, 256 + 128 * kind
            if kind:
                real, imag = real + share[w, :, 128:256], imag + share[w, :, 384:512]
            share[w, :, first : first + 128] = real
            share[w, :, second : second + 128] = imag
        return carry

    lax.fori_loop(0, gy_count, weigh, 0)

    def c_copy(w, b, slot):
        return pltpu.make_async_remote_copy(
            src_ref=share.at[w],
            dst_ref=share_in.at[b],
            send_sem=c_send.at[slot],
            recv_sem=c_recv.at[b],
            device_id=(gx, w),
            device_id_type=MESH,
        )

    for step in far_first(gy_count):
        c_copy(along_gy(step), gy, step).start()
    lax.fori_loop(0, gy_count, monitor_update, 0)

    def hand_out(z, carry):
        for c in range(3):
            electric_out[c, z] = field[c, z + 1, 0:8, :]
            magnetic_out[c, z] = field[3 + c, z + 1, 0:8, :]
        return carry

    lax.fori_loop(0, 16, hand_out, 0)
    loads[4].wait()
    slab_held = [[slab_records[c, s] for s in range(2)] for c in range(2)]

    def slab_update(i, carry):
        for j in range(4):
            f = 4 * i + j
            first, second = slab_table[0, f], slab_table[1, f]
            for c in range(2):
                slab_out[c, f] = slab_out[c, f] + (
                    first * slab_held[c][0] + second * slab_held[c][1]
                )
        return carry

    lax.fori_loop(0, slab_out.shape[1] // 4, slab_update, 0)

    for other in (0, 1):

        def take_m(step, carry):
            m_copy(along_gx(step), other, along_gx(-step), step).wait_recv()
            return carry

        lax.fori_loop(1 - other, gx_count, take_m, 0)
    for g in range(gx_count):
        xbuf[1, kept * g : kept * (g + 1), :] = kin_m[0, g] + kin_m[1, g]
    m_real, m_imag = x_sums(xbuf[1], xm_lead, xm_rest, 2)
    total = share[gy]
    for step in far_first(gy_count)[::-1]:
        b = along_gy(-step)
        c_copy(along_gy(step), b, step).wait_recv()
        total = total + share_in[b]

    for part, blocks in enumerate((m_real, m_imag)):
        for kind in range(2):
            first = 128 * (2 * part + kind)
            value = total[:, first : first + 128] + blocks[kind]
            for c in range(2):
                orders_out[0, part, 2 * kind + c] = value[:, c * OX : (c + 1) * OX]

    for copy in shares:
        copy.wait_send()

    def sent_y(step, carry):
        c_copy(along_gy(step), gy, step).wait_send()
        return carry

    def sent_x(step, carry):
        x_copy(kbuf_f, kin_f, f_send, f_recv, along_gx(step), gx, step).wait_send()
        x_copy(kbuf_h, kin_h, h_send, h_recv, along_gx(step), gx, step).wait_send()
        return carry

    for step in range(1, z_count):
        a_copy(along_z(step), zi, step).wait_send()
    for other in (1, 0):

        def sent_m(step, carry):
            m_copy(along_gx(step), other, None, step).wait_send()
            return carry

        lax.fori_loop(1 - other, gx_count, sent_m, 0)
    lax.fori_loop(1, gy_count, sent_y, 0)
    lax.fori_loop(1, gx_count, sent_x, 0)


def hand_over_kernel(*refs):
    count = len(refs) // 2
    copies = [
        pltpu.make_async_copy(source, target, refs[-1].at[i])
        for i, (source, target) in enumerate(zip(refs[:count], refs[count:-1]))
    ]
    for copy in copies:
        copy.start()
    for copy in copies:
        copy.wait()


def per_device(
    gx_count,
    gy_count,
    order_count,
    electric,
    magnetic,
    material,
    permittivity,
    slab_spectra,
    monitor_spectra,
    wave_index,
):
    freq_count = slab_spectra.shape[1] // 2
    kept = order_count // gx_count
    (y_lead, y_rest), y_turn = y_tables(gy_count, 128, order_count)
    xm_lead, xm_rest = x_local_table(gx_count, 8, 4, gy_count * 128)
    xf_lead, xf_rest = x_local_table(gx_count, 8, 8, gy_count * 128)
    x_turn = x_turn_table(gx_count, 8, kept)
    tables = [y_lead, y_rest, y_turn, xm_lead, xm_rest, xf_lead, xf_rest, x_turn]
    hbm = pl.BlockSpec(memory_space=pl.ANY)
    vmem = pl.BlockSpec(memory_space=pltpu.VMEM)
    smem = pl.BlockSpec(memory_space=pltpu.SMEM)
    f32 = jnp.float32
    dma = pltpu.SemaphoreType.DMA
    held = pl.pallas_call(
        functools.partial(whole_kernel, gx_count, gy_count),
        name="leapfrog_orders",
        out_shape=(
            pltpu.VMEM(electric.shape, f32),
            pltpu.VMEM(magnetic.shape, f32),
            pltpu.VMEM(slab_spectra.shape, f32),
            pltpu.VMEM(monitor_spectra.shape, f32),
            pltpu.VMEM((1, 2, 4, kept, OX), f32),
        ),
        in_specs=[hbm] * 13 + [smem] * 4,
        out_specs=(vmem,) * 5,
        scratch_shapes=[
            pltpu.VMEM((7, 18, 16, 128), f32),
            pltpu.VMEM((7, 16, 128), f32),
            pltpu.VMEM((16, 8, 128), jnp.int32),
            pltpu.VMEM((gy_count, 2, 4, 8, 128), f32),
            pltpu.VMEM((gy_count // 2, 2, 2, 3, 8, 128), f32),
            pltpu.VMEM((7, 8, 128), f32),
            pltpu.VMEM((2, 2, 8, 128), f32),
            pltpu.VMEM((8, 2, 8, 128), f32),
            pltpu.VMEM((2, 2, 2, 8, 128), f32),
            pltpu.VMEM((2, gx_count, kept, 128), f32),
            pltpu.VMEM((2, gx_count, kept, 128), f32),
            pltpu.VMEM((gx_count, kept, 128), f32),
            pltpu.VMEM((gx_count, kept, 128), f32),
            pltpu.VMEM((gx_count, kept, 16 * gy_count), f32),
            pltpu.VMEM((gx_count, kept, 16 * gy_count), f32),
            pltpu.VMEM((2, gx_count * kept, 128), f32),
            pltpu.VMEM((gy_count, kept, 512), f32),
            pltpu.VMEM((gy_count, kept, 512), f32),
            pltpu.VMEM((2, 4, 8, 128), f32),
            pltpu.VMEM((2, 2, 8, 128), f32),
        ]
        + [pltpu.VMEM(table.shape, table.dtype) for table in tables]
        + [
            dma((13,)),
            dma((2,)),
            dma((2,)),
            dma((8,)),
            dma((8,)),
            dma((gy_count // 2,)),
            dma((gy_count // 2,)),
            dma((2, gx_count)),
            dma((2, gx_count)),
            dma((gx_count,)),
            dma((gx_count,)),
            dma((gx_count,)),
            dma((gx_count,)),
            dma((gy_count,)),
            dma((gy_count,)),
        ],
        compiler_params=pltpu.CompilerParams(collective_id=0, has_side_effects=True),
    )(
        electric,
        magnetic,
        material,
        monitor_spectra,
        slab_spectra,
        *[jnp.asarray(table) for table in tables],
        permittivity,
        wave_index,
        jnp.asarray(monitor_weights(freq_count)),
        jnp.asarray(slab_weights(freq_count)),
    )
    electric_next, magnetic_next, slab_next, monitor_next, orders = pl.pallas_call(
        hand_over_kernel,
        name="hand_over",
        out_shape=tuple(jax.ShapeDtypeStruct(value.shape, f32) for value in held),
        in_specs=[vmem] * 5,
        out_specs=(hbm,) * 5,
        scratch_shapes=[dma((5,))],
    )(*[pltpu.with_memory_space_constraint(value, pltpu.VMEM) for value in held])
    return (
        electric_next,
        magnetic_next,
        slab_next,
        monitor_next,
        orders,
    )


def solution(mesh, order_count=128):
    fields = P(None, None, "gx", "gy")
    spectra = P(None, None, None, "gx", "gy")
    return jax.shard_map(
        functools.partial(per_device, mesh.shape["gx"], mesh.shape["gy"], order_count),
        mesh=mesh,
        in_specs=(fields, fields, P(None, "gx", "gy"), P(), fields, spectra, P()),
        out_specs=(fields, fields, fields, spectra, P("gy", None, None, "gx", None)),
        check_vma=False,
    )
```
